32 devices in a mesh: ctx: 8 (over y, x, core), kvh: 4 (over z).
Axes of the slice: x: 2, y: 2, z: 4, core: 2. Of those that a mesh axis runs over, the one named last changes fastest.
Arguments:
- query_heads: bfloat16 [16384, 4096], P('ctx', 'kvh'), may hold values from -8 to 8
- key_heads: bfloat16 [16384, 1024], P('ctx', 'kvh'), may hold values from -4.5 to 4.5
- value_head_rows: bfloat16 [16384, 1024], P('ctx', 'kvh'), may hold values from -6 to 6
- out_weight: bfloat16 [4096, 4096], P('kvh'), may hold values from -0.09375 to 0.09375
- piece_lengths: int32 [16], replicated, may hold values from 1 to 4096, 16384 in all
- block_order: int32 [128], replicated, may hold values from 0 to 127, as said below
Outputs:
- mixed: bfloat16 [16384, 4096], P(('ctx', 'kvh'))
The draws below stay inside these ranges and needn't reach their ends.
Inputs may be any that keep to these rules, and one draw needn't show every extreme that they name: `block_order`: a permutation of the blocks; slot d * 16 + s * 2 + j with 0 <= j < 2 holds a block of the contiguous range s * 16 to (s + 1) * 16 - 1. `piece_lengths`: they sum to 16384.
All inputs are finite; a program needn't handle non-finite values.
Results may differ from the reference program's by a relative error of at most 0.013.
Values may be sent and summed in bfloat16 or wider, within the bound.
A program may use at most 128 MiB of HBM per device.

```python
import math
import jax
import jax.numpy as jnp
import numpy as np
from jax import lax

D = 4096
QUERY_HEAD_COUNT = 32
KEY_VALUE_HEADS = 8
HEAD_SIZE = 128
BLK = 128
MOST = 4096
PACKED_TOKENS = 16384
NPIECE = 16
NBLK = 128
BPD = 16
PER = 2
N_CTX = 8
N_KVH = 4


def draw_key_heads(key, part):
    final_output = jnp.clip(jax.random.normal(jax.random.fold_in(key, 22), (PACKED_TOKENS, KEY_VALUE_HEADS * HEAD_SIZE), jnp.float32), -4.5, 4.5)
    return final_output.astype(jnp.bfloat16)


def draw_query_heads(key, part):
    final_output = jnp.clip(jax.random.normal(jax.random.fold_in(key, 24), (PACKED_TOKENS, QUERY_HEAD_COUNT * HEAD_SIZE), jnp.float32), -4.5, 4.5)
    return final_output.astype(jnp.bfloat16)


def shard_permutation(subkey):
    return jax.random.permutation(subkey, BPD)


def draw_block_order(key, part):
    subkeys = jax.random.split(jax.random.fold_in(key, 31), N_CTX)
    perms = jax.vmap(shard_permutation)(subkeys).astype(jnp.int32)
    shifted = perms.reshape(N_CTX, N_CTX, PER) + (jnp.arange(N_CTX, dtype=jnp.int32) * BPD)[:, None, None]
    return jnp.transpose(shifted, (1, 0, 2)).reshape(NBLK).astype(jnp.int32)


def block_levels(stream_key, shape, pieces, smallest, largest):
    loudness, own = 1.0, jax.random.fold_in(stream_key, 6)
    for position, blocks in pieces:
        steps = jnp.exp(jax.random.uniform(jax.random.fold_in(own, position), (blocks,), jnp.float32, smallest / len(pieces), largest / len(pieces)))
        loudness = loudness * jnp.repeat(steps, shape[position] // blocks).reshape([-1 if axis == position else 1 for axis in range(len(shape))])
    return loudness


def profile(number_of, total, reach, skew):
    loads = [(1 << 20) // math.isqrt(rank ** skew) + 1 for rank in range(2, number_of + 1)]
    spare, counts = total - reach - (number_of - 1), [1] * (number_of - 1)
    while spare > 0:
        free = [i for i in range(number_of - 1) if counts[i] < reach]
        whole, left = sum([loads[i] for i in free]), spare
        for i in free:
            more = min(reach - counts[i], max(1, left * loads[i] // whole), spare)
            counts[i] = counts[i] + more
            spare = spare - more
    return np.array([reach] + counts)


def uneven(key, number_of, total, limit, lean):
    if number_of == 2:
        one = jax.random.randint(key, (), max(1, total - limit), min(limit, total - 1) + 1)
        return jnp.stack([one, total - one])
    tallies = jnp.asarray(profile(number_of, total, limit, lean), jnp.int32)
    twos = (number_of - 1) // 2
    source_of, receiver = tallies[1:1 + 2 * twos:2], tallies[2:2 + 2 * twos:2]
    slack = jnp.minimum(source_of - 1, limit - receiver)
    moved = jax.random.randint(jax.random.fold_in(key, 1), (twos,), 0, 1 << 20) % (slack + 1)
    tallies = tallies.at[1:1 + 2 * twos:2].set(source_of - moved).at[2:2 + 2 * twos:2].set(receiver + moved)
    return tallies[jax.random.permutation(jax.random.fold_in(key, 2), number_of)]


def scatter_about(rng, shape, scale, most, cuts=(), kind=jnp.bfloat16):
    drawn = scale * jax.random.normal(rng, shape, jnp.float32)
    if cuts:
        drawn = drawn * block_levels(rng, shape, cuts, -0.22, 0.18)
    return jnp.clip(drawn, -most, most).astype(kind)


def setup_inputs(seed: int = 0) -> dict:
    streams_of = jax.random.split(jax.random.key(seed), 7)
    query_heads = draw_query_heads(jax.random.fold_in(streams_of[6], 71), 0)
    key_heads = draw_key_heads(jax.random.fold_in(streams_of[6], 71), 0)
    value_head_rows = scatter_about(streams_of[2], (PACKED_TOKENS, KEY_VALUE_HEADS * HEAD_SIZE), 1.0, 6.0, ((0, 8), (1, 4)))
    out_weight = scatter_about(streams_of[3], (QUERY_HEAD_COUNT * HEAD_SIZE, D), (QUERY_HEAD_COUNT * HEAD_SIZE) ** -0.5, 0.09375, ((0, 4),))
    piece_lengths = uneven(streams_of[4], NPIECE, PACKED_TOKENS, MOST, 2).astype(jnp.int32)
    block_order = draw_block_order(jax.random.fold_in(streams_of[6], 71), 0)
    return dict(query_heads=query_heads, key_heads=key_heads, value_head_rows=value_head_rows, out_weight=out_weight, piece_lengths=piece_lengths, block_order=block_order)


def piece_starts(positions, piece_lengths):
    piece_ends = jnp.cumsum(piece_lengths).astype(jnp.int32)
    chosen = jnp.where(piece_ends[None, :] <= positions[:, None], piece_lengths[None, :], 0)
    return jnp.sum(chosen, axis=1).astype(jnp.int32)


def attend(query_block, key_window, value_window, query_pos, key_pos, query_start):
    groups = key_window.shape[1] // HEAD_SIZE
    per_group = query_block.shape[1] // key_window.shape[1]
    query_four = query_block.reshape(query_block.shape[0], groups, per_group, HEAD_SIZE).astype(jnp.float32)
    key_three = key_window.reshape(-1, groups, HEAD_SIZE).astype(jnp.float32)
    value_three = value_window.reshape(-1, groups, HEAD_SIZE).astype(jnp.float32)
    scores = jnp.einsum("qgjd,kgd->gjqk", query_four, key_three) * (1.0 / (HEAD_SIZE ** 0.5))
    allowed = (key_pos[None, :] >= query_start[:, None]) & (key_pos[None, :] <= query_pos[:, None])
    masked = jnp.where(allowed, scores, -jnp.inf)
    highest = jnp.max(masked, axis=-1, keepdims=True)
    weights = jnp.exp(masked - highest)
    totals = jnp.sum(weights, axis=-1)
    rounded = weights.astype(jnp.bfloat16).astype(jnp.float32)
    summed = jnp.einsum("gjqk,kgd->qgjd", rounded, value_three)
    scaled = summed / jnp.transpose(totals, (2, 0, 1))[..., None]
    return scaled.reshape(query_block.shape[0], -1).astype(jnp.bfloat16)


def reference(query_heads, key_heads, value_head_rows, out_weight, piece_lengths, block_order):
    positions = jnp.arange(PACKED_TOKENS, dtype=jnp.int32)
    start_all = piece_starts(positions, piece_lengths)
    zero_rows = jnp.zeros((MOST, key_heads.shape[1]), jnp.bfloat16)
    key_padded = jnp.concatenate([zero_rows, key_heads], axis=0)
    value_padded = jnp.concatenate([zero_rows, value_head_rows], axis=0)
    offsets = jnp.arange(BLK, dtype=jnp.int32)
    window_offsets = jnp.arange(MOST + BLK, dtype=jnp.int32)

    def attend_one(block_id):
        first_row = (block_id * BLK).astype(jnp.int32)
        query_block = lax.dynamic_slice_in_dim(query_heads, first_row, BLK, 0)
        key_window = lax.dynamic_slice_in_dim(key_padded, first_row, MOST + BLK, 0)
        value_window = lax.dynamic_slice_in_dim(value_padded, first_row, MOST + BLK, 0)
        query_pos = first_row + offsets
        key_pos = first_row - MOST + window_offsets
        query_start = lax.dynamic_slice_in_dim(start_all, first_row, BLK, 0)
        return attend(query_block, key_window, value_window, query_pos, key_pos, query_start)

    attended = lax.map(attend_one, jnp.arange(NBLK, dtype=jnp.int32))
    arranged = jnp.take(attended, block_order, axis=0).reshape(PACKED_TOKENS, QUERY_HEAD_COUNT * HEAD_SIZE)
    width = QUERY_HEAD_COUNT * HEAD_SIZE // N_KVH
    final_output = jnp.zeros((PACKED_TOKENS, D), jnp.float32)
    for group_index in range(N_KVH):
        partial_sum = jnp.dot(arranged[:, group_index * width:(group_index + 1) * width],
                              out_weight[group_index * width:(group_index + 1) * width, :],
                              preferred_element_type=jnp.float32).astype(jnp.bfloat16)
        partial_sum = lax.optimization_barrier(partial_sum)
        final_output = final_output + partial_sum.astype(jnp.float32)
    return final_output.astype(jnp.bfloat16)
```

```python
import functools
import math
import jax
import jax.numpy as jnp
from jax import lax
from jax.experimental import pallas as pl
from jax.experimental.pallas import tpu as pltpu
from jax.sharding import Mesh, PartitionSpec as P

HEAD_SIZE = 128
BLK = 128
MOST = 4096
CHUNK = 1024
CTX = ("cg", "cp")
SCALE = math.log2(math.e) / HEAD_SIZE**0.5
NEG = -1e30


def attend_kernel(
    near, firsts, lows, p_first, p_last, p_start, q_at, o_at, side,
    q_ref, far_ref, kv0, kv1, kv2, kv3, out_ref,
    kv_ref, q_four, sbuf, top, acc, sems,
):
    step = pl.program_id(0)
    heads = q_ref.shape[1] // HEAD_SIZE
    shard = kv0.shape[0]

    @pl.when(step == 0)
    def _():
        copies = [
            pltpu.make_async_copy(
                src,
                kv_ref.at[pl.ds(pl.multiple_of((i // 2 * 2 + lax.rem(i + side[0], 2)) * shard, BLK), shard), :],
                sems.at[i],
            )
            for i, src in enumerate((kv0, kv1, kv2, kv3))
        ]
        for copy in copies:
            copy.start()
        for copy in copies:
            copy.wait()

    def stack(src):
        for h in range(heads):
            q_four[h * BLK : (h + 1) * BLK, :] = src[:, h * HEAD_SIZE : (h + 1) * HEAD_SIZE]

    @pl.when(step < near)
    def _():
        stack(q_ref)

    @pl.when(step >= near)
    def _():
        stack(far_ref)

    first = firsts[step]
    end = first + BLK
    count = (end - lows[step] + CHUNK - 1) // CHUNK
    pos = first + lax.broadcasted_iota(jnp.int32, (BLK, 1), 0)
    start = lax.fori_loop(
        p_first[step] + 1,
        p_last[step] + 1,
        lambda p, s: jnp.where(p_start[p] <= pos, p_start[p], s),
        jnp.full((BLK, 1), p_start[p_first[step]], jnp.int32),
    )
    latest = p_start[p_last[step]]
    wide = CHUNK // HEAD_SIZE

    def score(j, masked, init):
        begin = end - (j + 1) * CHUNK
        at = pl.multiple_of(jnp.maximum(begin, 0), BLK)
        keys = kv_ref[pl.ds(at, CHUNK), :HEAD_SIZE]
        s = lax.dot_general(
            q_four[...], keys, (((1,), (1,)), ((), ())), preferred_element_type=jnp.float32
        )
        if masked:
            key_pos = at + lax.broadcasted_iota(jnp.int32, (BLK, CHUNK), 1)
            allowed = (key_pos >= start) & (key_pos <= jnp.minimum(pos, begin + CHUNK - 1))
            s = jnp.where(jnp.concatenate([allowed] * heads, axis=0), s, NEG)
        sbuf[j] = s
        m = s[:, :HEAD_SIZE]
        for w in range(1, wide):
            m = jnp.maximum(m, s[:, w * HEAD_SIZE : (w + 1) * HEAD_SIZE])
        top[...] = m if init else jnp.maximum(top[...], m)

    score(0, True, True)

    def first_pass(j, carry):
        full = end - (j + 1) * CHUNK >= latest

        @pl.when(full)
        def _():
            score(j, False, False)

        @pl.when(jnp.logical_not(full))
        def _():
            score(j, True, False)

        return carry

    lax.fori_loop(1, count, first_pass, 0)
    top[...] = jnp.broadcast_to(jnp.max(top[...], axis=1, keepdims=True), top.shape)

    def mix(j, init):
        at = pl.multiple_of(jnp.maximum(end - (j + 1) * CHUNK, 0), BLK)
        values = kv_ref[pl.ds(at, CHUNK), HEAD_SIZE:]
        both = jnp.concatenate([values, jnp.ones_like(values)], axis=1)
        m = jnp.concatenate([top[...]] * wide, axis=1)
        weights = jnp.exp2((sbuf[j] - m) * SCALE).astype(jnp.bfloat16)
        r = jnp.dot(weights, both, preferred_element_type=jnp.float32)
        acc[...] = r if init else acc[...] + r

    mix(0, True)

    def second_pass(j, carry):
        mix(j, False)
        return carry

    lax.fori_loop(1, count, second_pass, 0)
    for h in range(heads):
        rows = slice(h * BLK, (h + 1) * BLK)
        out_ref[:, h * HEAD_SIZE : (h + 1) * HEAD_SIZE] = (
            acc[rows, :HEAD_SIZE] / acc[rows, HEAD_SIZE:]
        ).astype(jnp.bfloat16)


def attend(near, meta, query, far, pieces, g, width):
    rows = query.shape[0]
    stacked = BLK * width // HEAD_SIZE
    chunks = (MOST + BLK + CHUNK - 1) // CHUNK
    window = 4 * rows

    def near_block(i, *s):
        return s[5][jnp.minimum(i, near - 1)], g

    def far_block(i, *s):
        return s[5][jnp.maximum(i, min(near, rows // BLK - 1))], g

    return pl.pallas_call(
        functools.partial(attend_kernel, near),
        out_shape=jax.ShapeDtypeStruct((rows, width), jnp.bfloat16),
        grid_spec=pltpu.PrefetchScalarGridSpec(
            num_scalar_prefetch=8,
            grid=(rows // BLK,),
            in_specs=[
                pl.BlockSpec((BLK, width), near_block),
                pl.BlockSpec((BLK, width), far_block),
            ]
            + [pl.BlockSpec(memory_space=pl.ANY)] * 4,
            out_specs=pl.BlockSpec((BLK, width), lambda i, *s: (s[6][i], 0)),
            scratch_shapes=[
                pltpu.VMEM((window, 2 * HEAD_SIZE), jnp.bfloat16),
                pltpu.VMEM((stacked, HEAD_SIZE), jnp.bfloat16),
                pltpu.VMEM((chunks, stacked, CHUNK), jnp.float32),
                pltpu.VMEM((stacked, HEAD_SIZE), jnp.float32),
                pltpu.VMEM((stacked, 2 * HEAD_SIZE), jnp.float32),
                pltpu.SemaphoreType.DMA((4,)),
            ],
        ),
        compiler_params=pltpu.CompilerParams(vmem_limit_bytes=40 * 1024 * 1024),
        cost_estimate=pl.CostEstimate(
            flops=4 * rows * width * 2600, bytes_accessed=window * 512, transcendentals=rows * 4 * 2600
        ),
    )(*meta, query, far, *pieces)


def body(query_heads, key_heads, value_head_rows, out_weight, piece_lengths, block_order):
    num_ctx = lax.axis_size(CTX)
    num_cg = lax.axis_size("cg")
    num_kvh = lax.axis_size("kvh")
    chip = lax.axis_index("cg")
    core = lax.axis_index("cp")
    shard = query_heads.shape[0]
    block_count = shard // BLK
    per_pair = block_count // num_ctx
    groups = key_heads.shape[1] // HEAD_SIZE
    width = query_heads.shape[1] // groups
    pieces = piece_lengths.shape[0]
    swap = [(0, 1), (1, 0)]
    onward = [(i, i + 1) for i in range(num_cg - 1)]

    own = [
        jnp.concatenate([a[:, g * HEAD_SIZE : (g + 1) * HEAD_SIZE] for a in (key_heads, value_head_rows)], axis=1)
        for g in range(groups)
    ]
    windows = []
    for g in range(groups):
        before = lax.ppermute(own[g], "cg", onward)
        beside = lax.ppermute(own[g], "cp", swap)
        before_beside = lax.ppermute(before, "cp", swap)
        windows.append((before, before_beside, own[g], beside))
    far = lax.ppermute(query_heads, "cp", swap) if per_pair > 1 else query_heads

    steps = num_ctx * per_pair
    table = block_order.reshape(num_ctx, num_cg, 2 * per_pair)
    mine = lax.dynamic_index_in_dim(table, chip, 1, keepdims=False).reshape(num_ctx, per_pair, 2)
    mine = lax.dynamic_index_in_dim(mine, core, 2, keepdims=False)
    places = jnp.arange(steps, dtype=jnp.int32).reshape(num_ctx, per_pair)
    if per_pair > 1:
        flip = core == 1
        mine = jnp.where(flip, mine[:, ::-1], mine)
        places = jnp.where(flip, places[:, ::-1], places)
    blocks = mine.T.reshape(steps)
    places = places.T.reshape(steps)
    near = num_ctx if per_pair > 1 else steps

    row = lax.broadcasted_iota(jnp.int32, (pieces, pieces), 0)
    column = lax.broadcasted_iota(jnp.int32, (pieces, pieces), 1)
    ends = jnp.sum(jnp.where(column <= row, piece_lengths[None, :], 0), axis=1)
    base = (chip - 1) * (2 * shard)
    p_start = (ends - piece_lengths - base).astype(jnp.int32)
    first_rows = blocks * BLK
    p_first = jnp.sum((ends[None, :] <= first_rows[:, None]).astype(jnp.int32), axis=1)
    p_last = jnp.sum((ends[None, :] <= first_rows[:, None] + BLK - 1).astype(jnp.int32), axis=1)
    lows = jnp.sum(jnp.where(ends[None, :] <= first_rows[:, None], piece_lengths[None, :], 0), axis=1)
    lows = lows // BLK * BLK - base
    meta = [
        a.astype(jnp.int32)
        for a in (first_rows - base, lows, p_first, p_last, p_start, blocks % block_count, places, core[None])
    ]

    half = out_weight.shape[1] // 2
    part = width // num_cg
    mine_w = lax.dynamic_slice_in_dim(out_weight, core * half, half, 1)
    weights = []
    for g in range(groups):
        piece = lax.dynamic_slice_in_dim(mine_w, g * width + chip * part, part, 0)
        rows = lax.all_gather(piece, "kvh", axis=0, tiled=True)
        weights.append(lax.all_gather(rows, "cg", axis=0, tiled=True))

    own_x, other_x = [], []
    for g in range(groups):
        attended = attend(near, meta, query_heads, far, windows[g], g, width)
        spread = lax.all_to_all(attended, CTX, split_axis=0, concat_axis=0, tiled=True)
        rows = lax.all_to_all(spread, "kvh", split_axis=0, concat_axis=0, tiled=True)
        rows = rows.reshape(num_kvh, 2, per_pair, BLK, num_cg, part).transpose(2, 1, 3, 4, 0, 5)
        rows = rows.reshape(2 * per_pair * BLK, num_kvh * width)
        own_x.append(rows)
        other_x.append(lax.ppermute(rows, "cp", swap))

    def project(parts):
        total = 0.0
        for x, w in zip(parts, weights):
            total = total + jnp.dot(x, w, preferred_element_type=jnp.float32)
        return total.astype(jnp.bfloat16)

    back = lax.ppermute(project(other_x), "cp", swap)
    here = project(own_x)
    return jnp.where(
        core == 0,
        jnp.concatenate([here, back], axis=1),
        jnp.concatenate([back, here], axis=1),
    )


def solution(mesh):
    num_ctx, num_kvh = mesh.devices.shape
    split = Mesh(mesh.devices.reshape(num_ctx // 2, 2, num_kvh), ("cg", "cp", "kvh"))
    placed = (P(CTX, "kvh"), P(CTX, "kvh"), P(CTX, "kvh"), P("kvh", None), P(), P())
    return jax.shard_map(
        body, mesh=split, in_specs=placed, out_specs=P(("cg", "cp", "kvh"), None), check_vma=False
    )
```

```python
import functools
import math
import jax
import jax.numpy as jnp
from jax import lax
from jax.experimental import pallas as pl
from jax.experimental.pallas import tpu as pltpu
from jax.sharding import Mesh, PartitionSpec as P

HEAD_SIZE = 128
BLK = 128
MOST = 4096
CHUNK = 1024
CTX = ("cg", "cp")
SCALE = math.log2(math.e) / HEAD_SIZE**0.5
NEG = -1e30


def attend_kernel(
    near, group, firsts, lows, p_first, p_last, p_start, q_at, o_at, side,
    q_ref, far_ref, kv0, kv1, kv2, kv3, out_ref,
    kv_ref, q_four, sbuf, top, acc, sems,
):
    step = pl.program_id(0)
    heads = q_ref.shape[1] // HEAD_SIZE
    shard = kv0.shape[0]

    @pl.when(step == 0)
    def _():
        copies = [
            pltpu.make_async_copy(
                src.at[pl.ds(group * shard if i > 1 else 0, shard), :],
                kv_ref.at[pl.ds(pl.multiple_of((i // 2 * 2 + lax.rem(i + side[0], 2)) * shard, BLK), shard), :],
                sems.at[i],
            )
            for i, src in enumerate((kv0, kv1, kv2, kv3))
        ]
        for copy in copies:
            copy.start()
        for copy in copies:
            copy.wait()

    def stack(src):
        for h in range(heads):
            q_four[h * BLK : (h + 1) * BLK, :] = src[:, h * HEAD_SIZE : (h + 1) * HEAD_SIZE]

    @pl.when(step < near)
    def _():
        stack(q_ref)

    @pl.when(step >= near)
    def _():
        stack(far_ref)

    first = firsts[step]
    end = first + BLK
    count = (end - lows[step] + CHUNK - 1) // CHUNK
    pos = first + lax.broadcasted_iota(jnp.int32, (BLK, 1), 0)
    start = lax.fori_loop(
        p_first[step] + 1,
        p_last[step] + 1,
        lambda p, s: jnp.where(p_start[p] <= pos, p_start[p], s),
        jnp.full((BLK, 1), p_start[p_first[step]], jnp.int32),
    )
    latest = p_start[p_last[step]]
    wide = CHUNK // HEAD_SIZE

    def score(j, masked, init):
        begin = end - (j + 1) * CHUNK
        at = pl.multiple_of(jnp.maximum(begin, 0), BLK)
        keys = kv_ref[pl.ds(at, CHUNK), :HEAD_SIZE]
        s = lax.dot_general(
            q_four[...], keys, (((1,), (1,)), ((), ())), preferred_element_type=jnp.float32
        )
        if masked:
            key_pos = at + lax.broadcasted_iota(jnp.int32, (BLK, CHUNK), 1)
            allowed = (key_pos >= start) & (key_pos <= jnp.minimum(pos, begin + CHUNK - 1))
            s = jnp.where(jnp.concatenate([allowed] * heads, axis=0), s, NEG)
        sbuf[j] = s
        m = s[:, :HEAD_SIZE]
        for w in range(1, wide):
            m = jnp.maximum(m, s[:, w * HEAD_SIZE : (w + 1) * HEAD_SIZE])
        top[...] = m if init else jnp.maximum(top[...], m)

    score(0, True, True)

    def first_pass(j, carry):
        full = end - (j + 1) * CHUNK >= latest

        @pl.when(full)
        def _():
            score(j, False, False)

        @pl.when(jnp.logical_not(full))
        def _():
            score(j, True, False)

        return carry

    lax.fori_loop(1, count, first_pass, 0)
    top[...] = jnp.broadcast_to(jnp.max(top[...], axis=1, keepdims=True), top.shape)

    def mix(j, init):
        at = pl.multiple_of(jnp.maximum(end - (j + 1) * CHUNK, 0), BLK)
        values = kv_ref[pl.ds(at, CHUNK), HEAD_SIZE:]
        both = jnp.concatenate([values, jnp.ones_like(values)], axis=1)
        m = jnp.concatenate([top[...]] * wide, axis=1)
        weights = jnp.exp2((sbuf[j] - m) * SCALE).astype(jnp.bfloat16)
        r = jnp.dot(weights, both, preferred_element_type=jnp.float32)
        acc[...] = r if init else acc[...] + r

    mix(0, True)

    def second_pass(j, carry):
        mix(j, False)
        return carry

    lax.fori_loop(1, count, second_pass, 0)
    for h in range(heads):
        rows = slice(h * BLK, (h + 1) * BLK)
        out_ref[:, h * HEAD_SIZE : (h + 1) * HEAD_SIZE] = (
            acc[rows, :HEAD_SIZE] / acc[rows, HEAD_SIZE:]
        ).astype(jnp.bfloat16)


def attend(near, meta, query, far, pieces, g, width):
    rows = query.shape[0]
    stacked = BLK * width // HEAD_SIZE
    chunks = (MOST + BLK + CHUNK - 1) // CHUNK
    window = 4 * rows

    def near_block(i, *s):
        return s[5][jnp.minimum(i, near - 1)], g

    def far_block(i, *s):
        return s[5][jnp.maximum(i, min(near, rows // BLK - 1))], g

    return pl.pallas_call(
        functools.partial(attend_kernel, near, g),
        out_shape=jax.ShapeDtypeStruct((rows, width), jnp.bfloat16),
        grid_spec=pltpu.PrefetchScalarGridSpec(
            num_scalar_prefetch=8,
            grid=(rows // BLK,),
            in_specs=[
                pl.BlockSpec((BLK, width), near_block),
                pl.BlockSpec((BLK, width), far_block),
            ]
            + [pl.BlockSpec(memory_space=pl.ANY)] * 4,
            out_specs=pl.BlockSpec((BLK, width), lambda i, *s: (s[6][i], 0)),
            scratch_shapes=[
                pltpu.VMEM((window, 2 * HEAD_SIZE), jnp.bfloat16),
                pltpu.VMEM((stacked, HEAD_SIZE), jnp.bfloat16),
                pltpu.VMEM((chunks, stacked, CHUNK), jnp.float32),
                pltpu.VMEM((stacked, HEAD_SIZE), jnp.float32),
                pltpu.VMEM((stacked, 2 * HEAD_SIZE), jnp.float32),
                pltpu.SemaphoreType.DMA((4,)),
            ],
        ),
        compiler_params=pltpu.CompilerParams(vmem_limit_bytes=40 * 1024 * 1024),
        cost_estimate=pl.CostEstimate(
            flops=4 * rows * width * 8000, bytes_accessed=window * 512, transcendentals=rows * 4 * 2600
        ),
    )(*meta, query, far, *pieces)


def body(query_heads, key_heads, value_head_rows, out_weight, piece_lengths, block_order):
    num_ctx = lax.axis_size(CTX)
    num_cg = lax.axis_size("cg")
    num_kvh = lax.axis_size("kvh")
    chip = lax.axis_index("cg")
    core = lax.axis_index("cp")
    shard = query_heads.shape[0]
    block_count = shard // BLK
    per_pair = block_count // num_ctx
    groups = key_heads.shape[1] // HEAD_SIZE
    width = query_heads.shape[1] // groups
    pieces = piece_lengths.shape[0]
    swap = [(0, 1), (1, 0)]
    onward = [(i, i + 1) for i in range(num_cg - 1)]

    def pair_of(keys, values, g):
        cols = slice(g * HEAD_SIZE, (g + 1) * HEAD_SIZE)
        return jnp.concatenate([keys[:, cols], values[:, cols]], axis=1)

    own = [pair_of(key_heads, value_head_rows, g) for g in range(groups)]
    both = jnp.concatenate(own, axis=0)

    far = lax.ppermute(query_heads, "cp", swap) if per_pair > 1 else query_heads

    steps = num_ctx * per_pair
    table = block_order.reshape(num_ctx, num_cg, 2 * per_pair)
    mine = lax.dynamic_index_in_dim(table, chip, 1, keepdims=False).reshape(num_ctx, per_pair, 2)
    mine = lax.dynamic_index_in_dim(mine, core, 2, keepdims=False)
    places = jnp.arange(steps, dtype=jnp.int32).reshape(num_ctx, per_pair)
    if per_pair > 1:
        flip = core == 1
        mine = jnp.where(flip, mine[:, ::-1], mine)
        places = jnp.where(flip, places[:, ::-1], places)
    blocks = mine.T.reshape(steps)
    places = places.T.reshape(steps)
    near = num_ctx if per_pair > 1 else steps

    row = lax.broadcasted_iota(jnp.int32, (pieces, pieces), 0)
    column = lax.broadcasted_iota(jnp.int32, (pieces, pieces), 1)
    ends = jnp.sum(jnp.where(column <= row, piece_lengths[None, :], 0), axis=1)
    base = (chip - 1) * (2 * shard)
    p_start = (ends - piece_lengths - base).astype(jnp.int32)
    first_rows = blocks * BLK
    p_first = jnp.sum((ends[None, :] <= first_rows[:, None]).astype(jnp.int32), axis=1)
    p_last = jnp.sum((ends[None, :] <= first_rows[:, None] + BLK - 1).astype(jnp.int32), axis=1)
    lows = jnp.sum(jnp.where(ends[None, :] <= first_rows[:, None], piece_lengths[None, :], 0), axis=1)
    lows = lows // BLK * BLK - base
    meta = [
        a.astype(jnp.int32)
        for a in (first_rows - base, lows, p_first, p_last, p_start, blocks % block_count, places, core[None])
    ]

    def spread(attended):
        return lax.all_to_all(attended, CTX, split_axis=0, concat_axis=0, tiled=True)

    if not (num_cg == 4 and num_kvh == 4 and groups == 2):
        weights = lax.all_gather(out_weight, "kvh", axis=0, tiled=True)
        columns = []
        beside = lax.ppermute(both, "cp", swap)
        for g in range(groups):
            before = lax.ppermute(own[g], "cg", onward)
            window = [before, lax.ppermute(before, "cp", swap), both, beside]
            rows = spread(attend(near, meta, query_heads, far, window, g, width))
            rows = lax.all_to_all(rows, "kvh", split_axis=0, concat_axis=0, tiled=True)
            columns.append(rows.reshape(num_kvh, 2, per_pair, BLK, width).transpose(2, 1, 3, 0, 4))
        x = jnp.stack(columns, axis=4).reshape(2 * per_pair * BLK, -1)
        return jnp.dot(x, weights, preferred_element_type=jnp.float32).astype(jnp.bfloat16)

    tie = lax.optimization_barrier
    depth = out_weight.shape[0] // 8
    mine_w = lax.dynamic_slice_in_dim(out_weight, (chip * 2 + core) * depth, depth, 0)
    first_way = [(c * 2 + p, (c ^ (1 + p)) * 2 + p) for c in range(4) for p in range(2)]
    second_way = [(c * 2 + p, (c ^ (2 - p)) * 2 + p) for c in range(4) for p in range(2)]

    def from_plane(t):
        return lax.ppermute(mine_w, "kvh", [(i, (i + t) % 4) for i in range(4)])

    def one_way(block):
        return lax.ppermute(block, CTX, first_way)

    def other_way(block):
        return lax.ppermute(block, CTX, second_way)

    def pass_on(block):
        return lax.ppermute(block, "cp", swap)

    before = lax.ppermute(own[0], "cg", onward)
    w_1, w_3 = from_plane(1), from_plane(3)
    beside = pass_on(both)
    before_beside = pass_on(before)
    before, before_beside, beside, far, w_1, w_3, mine_w, own[1] = tie(
        (before, before_beside, beside, far, w_1, w_3, mine_w, own[1])
    )
    after = lax.ppermute(own[1], "cg", onward)
    w_2 = from_plane(2)
    same = jnp.concatenate([w_1, w_3], axis=0)
    one, two = one_way(same), other_way(same)
    attended = attend(near, meta, query_heads, far, (before, before_beside, both, beside), 0, width)
    attended, after, w_2, one, two, same = tie((attended, after, w_2, one, two, same))
    spread_0 = spread(attended)
    after_beside = pass_on(after)
    three = other_way(one)
    one_2, two_2 = one_way(w_2), other_way(w_2)
    one_b, two_b = pass_on(one), pass_on(two)
    attended = attend(near, meta, query_heads, far, (after, after_beside, both, beside), 1, width)
    attended, spread_0, three, one_2, two_2, one_b, two_b, same, w_2 = tie(
        (attended, spread_0, three, one_2, two_2, one_b, two_b, same, w_2)
    )
    spreads = [spread_0, spread(attended)]
    three_2 = other_way(one_2)
    weights = {}
    for planes, arrays in (
        ((1, 3), ((same, pass_on(same)), (one, one_b), (two, two_b), (three, pass_on(three)))),
        ((2,), tuple((w, pass_on(w)) for w in (w_2, one_2, two_2, three_2))),
    ):
        for name, pair in zip(("same", "one", "two", "three"), arrays):
            for other, block in enumerate(pair):
                weights[planes, name, other] = block

    level = lax.axis_index("kvh")
    rows = 2 * per_pair * BLK
    arrived = []
    for spread in spreads:
        arrived.append([spread])
        for t in range(1, num_kvh):
            sent = lax.dynamic_slice_in_dim(spread, lax.rem(level + t, num_kvh) * rows, rows, 0)
            arrived[-1].append(lax.ppermute(sent, "kvh", [(i, (i + t) % num_kvh) for i in range(num_kvh)]))
    return project(arrived, out_weight, weights, rows, per_pair)


TILE = 512


def project_kernel(n_x, parts, per_pair, x_at, w_at, *refs):
    x_in, (out_ref, x_ref, w_ref, x_sems, w_sems) = refs[:n_x], refs[-5:]
    w_in, own_w = refs[n_x:-6], refs[-6]
    n_w = len(parts)
    step = pl.program_id(0)
    width = x_in[0].shape[1]
    depth = own_w.shape[0] // 8
    own = own_w.shape[0]

    def tile_copies(n, slot):
        cols = pl.ds(pl.multiple_of(n * TILE, TILE), TILE)
        ins = [
            pltpu.make_async_copy(
                w_in[k].at[pl.ds(row, depth), cols],
                w_ref.at[slot, pl.ds(pl.multiple_of(w_at[i], depth), depth), :],
                w_sems.at[slot, i],
            )
            for i, (k, row) in enumerate(parts)
        ]
        ins.append(
            pltpu.make_async_copy(
                own_w.at[:, cols],
                w_ref.at[slot, pl.ds(pl.multiple_of(w_at[n_w], own), own), :],
                w_sems.at[slot, n_w],
            )
        )
        return ins

    def x_copies():
        ins = []
        for i, src in enumerate(x_in):
            for p in range(2):
                for j in range(per_pair):
                    row = pl.multiple_of(x_at[n_x + i] + (p * per_pair + j) * BLK, BLK)
                    ins.append(
                        pltpu.make_async_copy(
                            src.at[pl.ds(row, BLK), :],
                            x_ref.at[
                                pl.ds((j * 2 + p) * BLK, BLK),
                                pl.ds(pl.multiple_of(x_at[i], width), width),
                            ],
                            x_sems.at[i, p * per_pair + j],
                        )
                    )
        return ins

    slot = lax.rem(step, 2)

    @pl.when(step == 0)
    def _():
        ins = x_copies() + tile_copies(0, 0)
        for copy in ins:
            copy.start()
        for copy in ins[: 2 * per_pair * n_x]:
            copy.wait()

    @pl.when(step + 1 < pl.num_programs(0))
    def _():
        for copy in tile_copies(step + 1, 1 - slot):
            copy.start()

    for copy in tile_copies(step, slot):
        copy.wait()
    out_ref[...] = jnp.dot(x_ref[...], w_ref[slot], preferred_element_type=jnp.float32).astype(jnp.bfloat16)


def project(arrived, own_w, weights, rows, per_pair):
    level, chip, core = (lax.axis_index(n) for n in ("kvh", "cg", "cp"))
    groups = len(arrived)
    width = arrived[0][0].shape[1]
    x_in, x_col, x_row = [], [], []
    for g in range(groups):
        for t, block in enumerate(arrived[g]):
            x_in.append(block)
            x_col.append((lax.rem(level + 4 - t, 4) * groups + g) * width)
            x_row.append(level * rows if t == 0 else level * 0)
    w_in, w_row, parts = [], [], []
    depth = own_w.shape[0] // 8
    for (planes, name, other), block in weights.items():
        p = core ^ 1 if other else core
        c = chip ^ {"same": p * 0, "one": 1 + p, "two": 2 - p, "three": p * 0 + 3}[name]
        for i, t in enumerate(planes):
            parts.append((len(w_in), i * depth))
            w_row.append(lax.rem(level + 4 - t, 4) * own_w.shape[0] + (c * 2 + p) * depth)
        w_in.append(block)
    w_row.append(level * own_w.shape[0])
    total = own_w.shape[0] * 4
    out = own_w.shape[1]
    return pl.pallas_call(
        functools.partial(project_kernel, len(x_in), parts, per_pair),
        out_shape=jax.ShapeDtypeStruct((rows, out), jnp.bfloat16),
        grid_spec=pltpu.PrefetchScalarGridSpec(
            num_scalar_prefetch=2,
            grid=(out // TILE,),
            in_specs=[pl.BlockSpec(memory_space=pl.ANY)] * (len(x_in) + len(w_in) + 1),
            out_specs=pl.BlockSpec((rows, TILE), lambda n, *_: (0, n)),
            scratch_shapes=[
                pltpu.VMEM((rows, total), jnp.bfloat16),
                pltpu.VMEM((2, total, TILE), jnp.bfloat16),
                pltpu.SemaphoreType.DMA((len(x_in), 2 * per_pair)),
                pltpu.SemaphoreType.DMA((2, len(parts) + 1)),
            ],
        ),
        compiler_params=pltpu.CompilerParams(vmem_limit_bytes=40 * 1024 * 1024),
        cost_estimate=pl.CostEstimate(
            flops=2 * rows * total * out, bytes_accessed=2 * total * out, transcendentals=0
        ),
    )(jnp.stack(x_col + x_row).astype(jnp.int32), jnp.stack(w_row).astype(jnp.int32), *x_in, *w_in, own_w)


def solution(mesh):
    num_ctx, num_kvh = mesh.devices.shape
    split = Mesh(mesh.devices.reshape(num_ctx // 2, 2, num_kvh), ("cg", "cp", "kvh"))
    placed = (P(CTX, "kvh"), P(CTX, "kvh"), P(CTX, "kvh"), P("kvh", None), P(), P())
    return jax.shard_map(
        body, mesh=split, in_specs=placed, out_specs=P(("cg", "cp", "kvh"), None), check_vma=False
    )
```

```python
import functools
import math
import jax
import jax.numpy as jnp
from jax import lax
from jax.experimental import pallas as pl
from jax.experimental.pallas import tpu as pltpu
from jax.sharding import Mesh, PartitionSpec as P

HEAD_SIZE = 128
BLK = 128
MOST = 4096
CHUNK = 1024
CTX = ("cg", "cp")
SCALE = math.log2(math.e) / HEAD_SIZE**0.5
NEG = -1e30


def attend_kernel(
    group, firsts, lows, p_first, p_last, p_start, q_at, side,
    q_ref, kv0, kv1, kv2, kv3, out_ref,
    kv_ref, q_four, sbuf, top, acc, sems,
):
    step = pl.program_id(0)
    heads = q_ref.shape[1] // HEAD_SIZE
    shard = kv0.shape[0]

    @pl.when(step == 0)
    def _():
        copies = [
            pltpu.make_async_copy(
                src.at[pl.ds(group * shard if i > 1 else 0, shard), :],
                kv_ref.at[pl.ds(pl.multiple_of((i // 2 * 2 + lax.rem(i + side[0], 2)) * shard, BLK), shard), :],
                sems.at[i],
            )
            for i, src in enumerate((kv0, kv1, kv2, kv3))
        ]
        for copy in copies:
            copy.start()
        for copy in copies:
            copy.wait()

    for h in range(heads):
        q_four[h * BLK : (h + 1) * BLK, :] = q_ref[:, h * HEAD_SIZE : (h + 1) * HEAD_SIZE]

    first = firsts[step]
    end = first + BLK
    count = (end - lows[step] + CHUNK - 1) // CHUNK
    pos = first + lax.broadcasted_iota(jnp.int32, (BLK, 1), 0)
    start = lax.fori_loop(
        p_first[step] + 1,
        p_last[step] + 1,
        lambda p, s: jnp.where(p_start[p] <= pos, p_start[p], s),
        jnp.full((BLK, 1), p_start[p_first[step]], jnp.int32),
    )
    latest = p_start[p_last[step]]
    wide = CHUNK // HEAD_SIZE

    def score(j, masked, init):
        begin = end - (j + 1) * CHUNK
        at = pl.multiple_of(jnp.maximum(begin, 0), BLK)
        keys = kv_ref[pl.ds(at, CHUNK), :HEAD_SIZE]
        s = lax.dot_general(
            q_four[...], keys, (((1,), (1,)), ((), ())), preferred_element_type=jnp.float32
        )
        if masked:
            key_pos = at + lax.broadcasted_iota(jnp.int32, (BLK, CHUNK), 1)
            allowed = (key_pos >= start) & (key_pos <= jnp.minimum(pos, begin + CHUNK - 1))
            s = jnp.where(jnp.concatenate([allowed] * heads, axis=0), s, NEG)
        sbuf[j] = s
        m = s[:, :HEAD_SIZE]
        for w in range(1, wide):
            m = jnp.maximum(m, s[:, w * HEAD_SIZE : (w + 1) * HEAD_SIZE])
        top[...] = m if init else jnp.maximum(top[...], m)

    score(0, True, True)

    def first_pass(j, carry):
        full = end - (j + 1) * CHUNK >= latest

        @pl.when(full)
        def _():
            score(j, False, False)

        @pl.when(jnp.logical_not(full))
        def _():
            score(j, True, False)

        return carry

    lax.fori_loop(1, count, first_pass, 0)
    top[...] = jnp.broadcast_to(jnp.max(top[...], axis=1, keepdims=True), top.shape)

    def mix(j, init):
        at = pl.multiple_of(jnp.maximum(end - (j + 1) * CHUNK, 0), BLK)
        values = kv_ref[pl.ds(at, CHUNK), HEAD_SIZE:]
        both = jnp.concatenate([values, jnp.ones_like(values)], axis=1)
        m = jnp.concatenate([top[...]] * wide, axis=1)
        weights = jnp.exp2((sbuf[j] - m) * SCALE).astype(jnp.bfloat16)
        r = jnp.dot(weights, both, preferred_element_type=jnp.float32)
        acc[...] = r if init else acc[...] + r

    mix(0, True)

    def second_pass(j, carry):
        mix(j, False)
        return carry

    lax.fori_loop(1, count, second_pass, 0)
    for h in range(heads):
        rows = slice(h * BLK, (h + 1) * BLK)
        out_ref[:, h * HEAD_SIZE : (h + 1) * HEAD_SIZE] = (
            acc[rows, :HEAD_SIZE] / acc[rows, HEAD_SIZE:]
        ).astype(jnp.bfloat16)


def attend(meta, query, pieces, g, width):
    steps = meta[0].shape[0]
    stacked = BLK * width // HEAD_SIZE
    chunks = (MOST + BLK + CHUNK - 1) // CHUNK
    window = 4 * query.shape[0]
    return pl.pallas_call(
        functools.partial(attend_kernel, g),
        out_shape=jax.ShapeDtypeStruct((steps * BLK, width), jnp.bfloat16),
        grid_spec=pltpu.PrefetchScalarGridSpec(
            num_scalar_prefetch=7,
            grid=(steps,),
            in_specs=[pl.BlockSpec((BLK, width), lambda i, *s: (s[5][i], g))]
            + [pl.BlockSpec(memory_space=pl.ANY)] * 4,
            out_specs=pl.BlockSpec((BLK, width), lambda i, *s: (i, 0)),
            scratch_shapes=[
                pltpu.VMEM((window, 2 * HEAD_SIZE), jnp.bfloat16),
                pltpu.VMEM((stacked, HEAD_SIZE), jnp.bfloat16),
                pltpu.VMEM((chunks, stacked, CHUNK), jnp.float32),
                pltpu.VMEM((stacked, HEAD_SIZE), jnp.float32),
                pltpu.VMEM((stacked, 2 * HEAD_SIZE), jnp.float32),
                pltpu.SemaphoreType.DMA((4,)),
            ],
        ),
        compiler_params=pltpu.CompilerParams(vmem_limit_bytes=60 * 1024 * 1024),
        cost_estimate=pl.CostEstimate(
            flops=4 * steps * BLK * width * 8000,
            bytes_accessed=window * 512,
            transcendentals=steps * BLK * 4 * 2600,
        ),
    )(*meta, query, *pieces)


def body(query_heads, key_heads, value_head_rows, out_weight, piece_lengths, block_order):
    num_ctx = lax.axis_size(CTX)
    num_cg = lax.axis_size("cg")
    num_kvh = lax.axis_size("kvh")
    chip = lax.axis_index("cg")
    core = lax.axis_index("cp")
    shard = query_heads.shape[0]
    block_count = shard // BLK
    per_pair = block_count // num_ctx
    groups = key_heads.shape[1] // HEAD_SIZE
    width = query_heads.shape[1] // groups
    pieces = piece_lengths.shape[0]
    swap = [(0, 1), (1, 0)]
    onward = [(i, i + 1) for i in range(num_cg - 1)]

    def pair_of(keys, values, g):
        cols = slice(g * HEAD_SIZE, (g + 1) * HEAD_SIZE)
        return jnp.concatenate([keys[:, cols], values[:, cols]], axis=1)

    own = [pair_of(key_heads, value_head_rows, g) for g in range(groups)]
    both = jnp.concatenate(own, axis=0)

    table = block_order.reshape(num_ctx, num_cg, 2 * per_pair)
    mine = lax.dynamic_index_in_dim(table, chip, 1, keepdims=False).reshape(num_ctx, per_pair, 2)
    mine = lax.dynamic_index_in_dim(mine, core, 2, keepdims=False)
    if per_pair > 1:
        mine = jnp.where(core == 1, mine[:, ::-1], mine)

    row = lax.broadcasted_iota(jnp.int32, (pieces, pieces), 0)
    column = lax.broadcasted_iota(jnp.int32, (pieces, pieces), 1)
    ends = jnp.sum(jnp.where(column <= row, piece_lengths[None, :], 0), axis=1)
    base = (chip - 1) * (2 * shard)
    p_start = (ends - piece_lengths - base).astype(jnp.int32)

    def meta_of(blocks):
        first_rows = blocks * BLK
        p_first = jnp.sum((ends[None, :] <= first_rows[:, None]).astype(jnp.int32), axis=1)
        p_last = jnp.sum((ends[None, :] <= first_rows[:, None] + BLK - 1).astype(jnp.int32), axis=1)
        lows = jnp.sum(jnp.where(ends[None, :] <= first_rows[:, None], piece_lengths[None, :], 0), axis=1)
        lows = lows // BLK * BLK - base
        parts = (first_rows - base, lows, p_first, p_last, p_start, blocks % block_count, core[None])
        return [a.astype(jnp.int32) for a in parts]

    def spread(attended):
        return lax.all_to_all(attended, CTX, split_axis=0, concat_axis=0, tiled=True)

    if not (num_cg == 4 and num_kvh == 4 and groups == 2 and per_pair == 2):
        weights = lax.all_gather(out_weight, "kvh", axis=0, tiled=True)
        beside = lax.ppermute(both, "cp", swap)
        queries = [query_heads] + [lax.ppermute(query_heads, "cp", swap)] * (per_pair - 1)
        columns = []
        for g in range(groups):
            before = lax.ppermute(own[g], "cg", onward)
            window = [before, lax.ppermute(before, "cp", swap), both, beside]
            found = [attend(meta_of(mine[:, i]), q, window, g, width) for i, q in enumerate(queries)]
            if per_pair > 1:
                found = [jnp.where(core == 1, b, a) for a, b in (found, found[::-1])]
            rows = jnp.stack([f.reshape(num_ctx, BLK, width) for f in found], axis=1)
            rows = spread(rows.reshape(-1, width))
            rows = lax.all_to_all(rows, "kvh", split_axis=0, concat_axis=0, tiled=True)
            columns.append(rows.reshape(num_kvh, 2, per_pair, BLK, width).transpose(2, 1, 3, 0, 4))
        x = jnp.stack(columns, axis=4).reshape(2 * per_pair * BLK, -1)
        return jnp.dot(x, weights, preferred_element_type=jnp.float32).astype(jnp.bfloat16)

    tie = lax.optimization_barrier
    depth = out_weight.shape[0] // 8
    mine_w = lax.dynamic_slice_in_dim(out_weight, (chip * 2 + core) * depth, depth, 0)
    first_way = [(c * 2 + p, (c ^ (1 + p)) * 2 + p) for c in range(4) for p in range(2)]
    second_way = [(c * 2 + p, (c ^ (2 - p)) * 2 + p) for c in range(4) for p in range(2)]

    def from_plane(t):
        return lax.ppermute(mine_w, "kvh", [(i, (i + t) % 4) for i in range(4)])

    def one_way(block):
        return lax.ppermute(block, CTX, first_way)

    def other_way(block):
        return lax.ppermute(block, CTX, second_way)

    def pass_on(block):
        return lax.ppermute(block, "cp", swap)

    near, far_meta = meta_of(mine[:, 0]), meta_of(mine[:, 1])
    level = lax.axis_index("kvh")
    rows = 2 * BLK

    def over_z(block):
        came = []
        for t in range(1, 4):
            sent = lax.dynamic_slice_in_dim(block, lax.rem(level + t, 4) * rows, rows, 0)
            came.append(lax.ppermute(sent, "kvh", [(i, (i + t) % 4) for i in range(4)]))
        return block, came

    before = lax.ppermute(own[0], "cg", onward)
    w_1 = from_plane(1)
    beside = pass_on(both)
    far = pass_on(query_heads)
    before, own[1] = tie((before, own[1]))
    after = lax.ppermute(own[1], "cg", onward)
    before_beside = pass_on(before)
    before, before_beside, beside, far, w_1, mine_w = tie((before, before_beside, beside, far, w_1, mine_w))
    w_3 = from_plane(3)
    one_1, two_1 = one_way(w_1), other_way(w_1)
    att_0 = attend(near, query_heads, (before, before_beside, both, beside), 0, width)

    att_0, after, w_3, mine_w, far, before = tie((att_0, after, w_3, mine_w, far, before))
    spread_0 = spread(att_0)
    after_beside = pass_on(after)
    w_2 = from_plane(2)
    one_3 = one_way(w_3)
    att_1 = attend(far_meta, far, (before, before_beside, both, beside), 0, width)

    att_1, spread_0, after, after_beside, one_1, two_1, w_1, w_3, one_3 = tie(
        (att_1, spread_0, after, after_beside, one_1, two_1, w_1, w_3, one_3)
    )
    spread_1 = spread(att_1)
    mixed_1 = other_way(jnp.concatenate([one_1, w_3], axis=0))
    kept_0, came_0 = over_z(spread_0)
    att_2 = attend(near, query_heads, (after, after_beside, both, beside), 1, width)

    att_2, came_0, spread_1, one_3, w_2, after = tie((att_2, came_0, spread_1, one_3, w_2, after))
    spread_2 = spread(att_2)
    kept_1, came_1 = over_z(spread_1)
    one_2 = one_way(w_2)
    att_3 = attend(far_meta, far, (after, after_beside, both, beside), 1, width)

    att_3, came_1, spread_2, one_2, mixed_1, one_3, w_2 = tie(
        (att_3, came_1, spread_2, one_2, mixed_1, one_3, w_2)
    )
    spread_3 = spread(att_3)
    kept_2, came_2 = over_z(spread_2)
    mixed_3 = other_way(jnp.concatenate([one_3, w_2], axis=0))
    three_2 = other_way(one_2)

    came_2, spread_3 = tie((came_2, spread_3))
    kept_3, came_3 = over_z(spread_3)
    mixed_3, three_2, w_1, one_1, two_1, mixed_1, w_3, one_3, w_2, one_2, spread_3 = tie(
        (mixed_3, three_2, w_1, one_1, two_1, mixed_1, w_3, one_3, w_2, one_2, spread_3)
    )
    weights = [
        (w_1, pass_on(w_1), [(1, 0)]),
        (one_1, pass_on(one_1), [(1, 1)]),
        (two_1, pass_on(two_1), [(1, 2)]),
        (mixed_1, pass_on(mixed_1), [(1, 3), (3, 2)]),
        (w_3, pass_on(w_3), [(3, 0)]),
        (one_3, pass_on(one_3), [(3, 1)]),
        (mixed_3, pass_on(mixed_3), [(3, 3), (2, 2)]),
        (w_2, pass_on(w_2), [(2, 0)]),
        (one_2, pass_on(one_2), [(2, 1)]),
        (three_2, pass_on(three_2), [(2, 3)]),
    ]
    parts = []
    for n, (kept, came) in enumerate(((kept_0, came_0), (kept_1, came_1), (kept_2, came_2), (kept_3, came_3))):
        parts.append((n // 2, n % 2, 0, kept, level * rows))
        parts += [(n // 2, n % 2, t, block, 0) for t, block in enumerate(came, 1)]
    return project(parts, out_weight, weights, width)


TILE = 512


def project_kernel(x_parts, parts, x_at, w_at, *refs):
    n_in = 1 + max(k for k, _ in x_parts)
    x_in, (out_ref, x_ref, w_ref, x_sems, w_sems) = refs[:n_in], refs[-5:]
    w_in, own_w = refs[n_in:-6], refs[-6]
    n_x, n_w = len(x_parts), len(parts)
    step = pl.program_id(0)
    width = x_in[0].shape[1]
    depth = own_w.shape[0] // 8
    own = own_w.shape[0]

    def tile_copies(n, slot):
        cols = pl.ds(pl.multiple_of(n * TILE, TILE), TILE)
        ins = [
            pltpu.make_async_copy(
                w_in[k].at[pl.ds(row, depth), cols],
                w_ref.at[slot, pl.ds(pl.multiple_of(w_at[i], depth), depth), :],
                w_sems.at[slot, i],
            )
            for i, (k, row) in enumerate(parts)
        ]
        ins.append(
            pltpu.make_async_copy(
                own_w.at[:, cols],
                w_ref.at[slot, pl.ds(pl.multiple_of(w_at[n_w], own), own), :],
                w_sems.at[slot, n_w],
            )
        )
        return ins

    def x_copies():
        ins = []
        for i, (k, half) in enumerate(x_parts):
            for p in range(2):
                row = pl.multiple_of(x_at[n_x + i] + p * BLK, BLK)
                to = ((p ^ half) * 2 + p) * BLK
                ins.append(
                    pltpu.make_async_copy(
                        x_in[k].at[pl.ds(row, BLK), :],
                        x_ref.at[pl.ds(to, BLK), pl.ds(pl.multiple_of(x_at[i], width), width)],
                        x_sems.at[i, p],
                    )
                )
        return ins

    slot = lax.rem(step, 2)

    @pl.when(step == 0)
    def _():
        ins = x_copies() + tile_copies(0, 0)
        for copy in ins:
            copy.start()
        for copy in ins[: 2 * n_x]:
            copy.wait()

    @pl.when(step + 1 < pl.num_programs(0))
    def _():
        for copy in tile_copies(step + 1, 1 - slot):
            copy.start()

    for copy in tile_copies(step, slot):
        copy.wait()
    out_ref[...] = jnp.dot(x_ref[...], w_ref[slot], preferred_element_type=jnp.float32).astype(jnp.bfloat16)


def project(found, own_w, weights, width):
    level, chip, core = (lax.axis_index(n) for n in ("kvh", "cg", "cp"))
    groups = own_w.shape[0] // width
    x_in, x_parts, x_col, x_row = [], [], [], []
    for g, half, t, block, row in found:
        place = [k for k, b in enumerate(x_in) if b is block]
        if not place:
            place = [len(x_in)]
            x_in.append(block)
        x_parts.append((place[0], half))
        x_col.append((lax.rem(level + 4 - t, 4) * groups + g) * width)
        x_row.append(row + level * 0)
    w_in, w_row, parts = [], [], []
    depth = own_w.shape[0] // 8
    for *blocks, content in weights:
        for other, block in enumerate(blocks):
            p = core ^ 1 if other else core
            for i, (t, way) in enumerate(content):
                c = chip ^ (p * 0, 1 + p, 2 - p, p * 0 + 3)[way]
                parts.append((len(w_in), i * depth))
                w_row.append(lax.rem(level + 4 - t, 4) * own_w.shape[0] + (c * 2 + p) * depth)
            w_in.append(block)
    w_row.append(level * own_w.shape[0])
    total = own_w.shape[0] * 4
    out = own_w.shape[1]
    rows = 4 * BLK
    return pl.pallas_call(
        functools.partial(project_kernel, x_parts, parts),
        out_shape=jax.ShapeDtypeStruct((rows, out), jnp.bfloat16),
        grid_spec=pltpu.PrefetchScalarGridSpec(
            num_scalar_prefetch=2,
            grid=(out // TILE,),
            in_specs=[pl.BlockSpec(memory_space=pl.ANY)] * (len(x_in) + len(w_in) + 1),
            out_specs=pl.BlockSpec((rows, TILE), lambda n, *_: (0, n)),
            scratch_shapes=[
                pltpu.VMEM((rows, total), jnp.bfloat16),
                pltpu.VMEM((2, total, TILE), jnp.bfloat16),
                pltpu.SemaphoreType.DMA((len(x_parts), 2)),
                pltpu.SemaphoreType.DMA((2, len(parts) + 1)),
            ],
        ),
        compiler_params=pltpu.CompilerParams(vmem_limit_bytes=60 * 1024 * 1024),
        cost_estimate=pl.CostEstimate(
            flops=2 * rows * total * out, bytes_accessed=2 * total * out, transcendentals=0
        ),
    )(jnp.stack(x_col + x_row).astype(jnp.int32), jnp.stack(w_row).astype(jnp.int32), *x_in, *w_in, own_w)


def solution(mesh):
    num_ctx, num_kvh = mesh.devices.shape
    split = Mesh(mesh.devices.reshape(num_ctx // 2, 2, num_kvh), ("cg", "cp", "kvh"))
    placed = (P(CTX, "kvh"), P(CTX, "kvh"), P(CTX, "kvh"), P("kvh", None), P(), P())
    return jax.shard_map(
        body, mesh=split, in_specs=placed, out_specs=P(("cg", "cp", "kvh"), None), check_vma=False
    )
```

```python
import functools
import math
import jax
import jax.numpy as jnp
from jax import lax
from jax.experimental import pallas as pl
from jax.experimental.pallas import tpu as pltpu
from jax.sharding import Mesh, PartitionSpec as P

HEAD_SIZE = 128
BLK = 128
MOST = 4096
CHUNK = 1024
CTX = ("cg", "cp")
SCALE = math.log2(math.e) / HEAD_SIZE**0.5
NEG = -1e30


def attend_kernel(
    group, firsts, lows, p_first, p_last, p_start, q_at, side,
    q_ref, kv0, kv1, kv2, kv3, out_ref,
    kv_ref, q_four, sbuf, top, acc, sems,
):
    step = pl.program_id(0)
    heads = q_ref.shape[1] // HEAD_SIZE
    shard = kv0.shape[0]

    @pl.when(step == 0)
    def _():
        copies = [
            pltpu.make_async_copy(
                src.at[pl.ds(group * shard if i > 1 else 0, shard), :],
                kv_ref.at[pl.ds(pl.multiple_of((i // 2 * 2 + lax.rem(i + side[0], 2)) * shard, BLK), shard), :],
                sems.at[i],
            )
            for i, src in enumerate((kv0, kv1, kv2, kv3))
        ]
        for copy in copies:
            copy.start()
        for copy in copies:
            copy.wait()

    for h in range(heads):
        q_four[h * BLK : (h + 1) * BLK, :] = q_ref[:, h * HEAD_SIZE : (h + 1) * HEAD_SIZE]

    first = firsts[step]
    end = first + BLK
    count = (end - lows[step] + CHUNK - 1) // CHUNK
    pos = first + lax.broadcasted_iota(jnp.int32, (BLK, 1), 0)
    start = lax.fori_loop(
        p_first[step] + 1,
        p_last[step] + 1,
        lambda p, s: jnp.where(p_start[p] <= pos, p_start[p], s),
        jnp.full((BLK, 1), p_start[p_first[step]], jnp.int32),
    )
    latest = p_start[p_last[step]]
    wide = CHUNK // HEAD_SIZE

    def score(j, masked, init):
        begin = end - (j + 1) * CHUNK
        at = pl.multiple_of(jnp.maximum(begin, 0), BLK)
        keys = kv_ref[pl.ds(at, CHUNK), :HEAD_SIZE]
        s = lax.dot_general(
            q_four[...], keys, (((1,), (1,)), ((), ())), preferred_element_type=jnp.float32
        )
        if masked:
            key_pos = at + lax.broadcasted_iota(jnp.int32, (BLK, CHUNK), 1)
            allowed = (key_pos >= start) & (key_pos <= jnp.minimum(pos, begin + CHUNK - 1))
            s = jnp.where(jnp.concatenate([allowed] * heads, axis=0), s, NEG)
        sbuf[j] = s
        m = s[:, :HEAD_SIZE]
        for w in range(1, wide):
            m = jnp.maximum(m, s[:, w * HEAD_SIZE : (w + 1) * HEAD_SIZE])
        top[...] = m if init else jnp.maximum(top[...], m)

    score(0, True, True)

    def first_pass(j, carry):
        full = end - (j + 1) * CHUNK >= latest

        @pl.when(full)
        def _():
            score(j, False, False)

        @pl.when(jnp.logical_not(full))
        def _():
            score(j, True, False)

        return carry

    lax.fori_loop(1, count, first_pass, 0)
    top[...] = jnp.broadcast_to(jnp.max(top[...], axis=1, keepdims=True), top.shape)

    def mix(j, init):
        at = pl.multiple_of(jnp.maximum(end - (j + 1) * CHUNK, 0), BLK)
        values = kv_ref[pl.ds(at, CHUNK), HEAD_SIZE:]
        both = jnp.concatenate([values, jnp.ones_like(values)], axis=1)
        m = jnp.concatenate([top[...]] * wide, axis=1)
        weights = jnp.exp2((sbuf[j] - m) * SCALE).astype(jnp.bfloat16)
        r = jnp.dot(weights, both, preferred_element_type=jnp.float32)
        acc[...] = r if init else acc[...] + r

    mix(0, True)

    def second_pass(j, carry):
        mix(j, False)
        return carry

    lax.fori_loop(1, count, second_pass, 0)
    for h in range(heads):
        rows = slice(h * BLK, (h + 1) * BLK)
        out_ref[:, h * HEAD_SIZE : (h + 1) * HEAD_SIZE] = (
            acc[rows, :HEAD_SIZE] / acc[rows, HEAD_SIZE:]
        ).astype(jnp.bfloat16)


def attend(meta, query, pieces, g, width):
    steps = meta[0].shape[0]
    stacked = BLK * width // HEAD_SIZE
    chunks = (MOST + BLK + CHUNK - 1) // CHUNK
    window = 4 * query.shape[0]
    return pl.pallas_call(
        functools.partial(attend_kernel, g),
        out_shape=jax.ShapeDtypeStruct((steps * BLK, width), jnp.bfloat16),
        grid_spec=pltpu.PrefetchScalarGridSpec(
            num_scalar_prefetch=7,
            grid=(steps,),
            in_specs=[pl.BlockSpec((BLK, width), lambda i, *s: (s[5][i], g))]
            + [pl.BlockSpec(memory_space=pl.ANY)] * 4,
            out_specs=pl.BlockSpec((BLK, width), lambda i, *s: (i, 0)),
            scratch_shapes=[
                pltpu.VMEM((window, 2 * HEAD_SIZE), jnp.bfloat16),
                pltpu.VMEM((stacked, HEAD_SIZE), jnp.bfloat16),
                pltpu.VMEM((chunks, stacked, CHUNK), jnp.float32),
                pltpu.VMEM((stacked, HEAD_SIZE), jnp.float32),
                pltpu.VMEM((stacked, 2 * HEAD_SIZE), jnp.float32),
                pltpu.SemaphoreType.DMA((4,)),
            ],
        ),
        compiler_params=pltpu.CompilerParams(vmem_limit_bytes=60 * 1024 * 1024),
        cost_estimate=pl.CostEstimate(
            flops=4 * steps * BLK * width * 8000,
            bytes_accessed=window * 512,
            transcendentals=steps * BLK * 4 * 2600,
        ),
    )(*meta, query, *pieces)


def body(query_heads, key_heads, value_head_rows, out_weight, piece_lengths, block_order):
    num_ctx = lax.axis_size(CTX)
    num_cg = lax.axis_size("cg")
    num_kvh = lax.axis_size("kvh")
    chip = lax.axis_index("cg")
    core = lax.axis_index("cp")
    shard = query_heads.shape[0]
    block_count = shard // BLK
    per_pair = block_count // num_ctx
    groups = key_heads.shape[1] // HEAD_SIZE
    width = query_heads.shape[1] // groups
    pieces = piece_lengths.shape[0]
    swap = [(0, 1), (1, 0)]
    onward = [(i, i + 1) for i in range(num_cg - 1)]

    def pair_of(keys, values, g):
        cols = slice(g * HEAD_SIZE, (g + 1) * HEAD_SIZE)
        return jnp.concatenate([keys[:, cols], values[:, cols]], axis=1)

    own = [pair_of(key_heads, value_head_rows, g) for g in range(groups)]
    both = jnp.concatenate(own, axis=0)

    table = block_order.reshape(num_ctx, num_cg, 2 * per_pair)
    mine = lax.dynamic_index_in_dim(table, chip, 1, keepdims=False).reshape(num_ctx, per_pair, 2)
    mine = lax.dynamic_index_in_dim(mine, core, 2, keepdims=False)
    if per_pair > 1:
        mine = jnp.where(core == 1, mine[:, ::-1], mine)

    row = lax.broadcasted_iota(jnp.int32, (pieces, pieces), 0)
    column = lax.broadcasted_iota(jnp.int32, (pieces, pieces), 1)
    ends = jnp.sum(jnp.where(column <= row, piece_lengths[None, :], 0), axis=1)
    base = (chip - 1) * (2 * shard)
    p_start = (ends - piece_lengths - base).astype(jnp.int32)

    def meta_of(blocks):
        first_rows = blocks * BLK
        p_first = jnp.sum((ends[None, :] <= first_rows[:, None]).astype(jnp.int32), axis=1)
        p_last = jnp.sum((ends[None, :] <= first_rows[:, None] + BLK - 1).astype(jnp.int32), axis=1)
        lows = jnp.sum(jnp.where(ends[None, :] <= first_rows[:, None], piece_lengths[None, :], 0), axis=1)
        lows = lows // BLK * BLK - base
        parts = (first_rows - base, lows, p_first, p_last, p_start, blocks % block_count, core[None])
        return [a.astype(jnp.int32) for a in parts]

    def spread(attended):
        return lax.all_to_all(attended, CTX, split_axis=0, concat_axis=0, tiled=True)

    if not (num_cg == 4 and num_kvh == 4 and groups == 2 and per_pair == 2):
        weights = lax.all_gather(out_weight, "kvh", axis=0, tiled=True)
        beside = lax.ppermute(both, "cp", swap)
        queries = [query_heads] + [lax.ppermute(query_heads, "cp", swap)] * (per_pair - 1)
        columns = []
        for g in range(groups):
            before = lax.ppermute(own[g], "cg", onward)
            window = [before, lax.ppermute(before, "cp", swap), both, beside]
            found = [attend(meta_of(mine[:, i]), q, window, g, width) for i, q in enumerate(queries)]
            if per_pair > 1:
                found = [jnp.where(core == 1, b, a) for a, b in (found, found[::-1])]
            rows = jnp.stack([f.reshape(num_ctx, BLK, width) for f in found], axis=1)
            rows = spread(rows.reshape(-1, width))
            rows = lax.all_to_all(rows, "kvh", split_axis=0, concat_axis=0, tiled=True)
            columns.append(rows.reshape(num_kvh, 2, per_pair, BLK, width).transpose(2, 1, 3, 0, 4))
        x = jnp.stack(columns, axis=4).reshape(2 * per_pair * BLK, -1)
        return jnp.dot(x, weights, preferred_element_type=jnp.float32).astype(jnp.bfloat16)

    tie = lax.optimization_barrier
    depth = out_weight.shape[0] // 8
    mine_w = lax.dynamic_slice_in_dim(out_weight, (chip * 2 + core) * depth, depth, 0)
    first_way = [(c * 2 + p, (c ^ (1 + p)) * 2 + p) for c in range(4) for p in range(2)]
    second_way = [(c * 2 + p, (c ^ (2 - p)) * 2 + p) for c in range(4) for p in range(2)]

    def from_plane(t):
        return lax.ppermute(mine_w, "kvh", [(i, (i + t) % 4) for i in range(4)])

    def one_way(block):
        return lax.ppermute(block, CTX, first_way)

    def other_way(block):
        return lax.ppermute(block, CTX, second_way)

    def pass_on(block):
        return lax.ppermute(block, "cp", swap)

    near, far_meta = meta_of(mine[:, 0]), meta_of(mine[:, 1])
    level = lax.axis_index("kvh")
    rows = 2 * BLK

    def over_z(block):
        came = []
        for t in range(1, 4):
            sent = lax.dynamic_slice_in_dim(block, lax.rem(level + t, 4) * rows, rows, 0)
            came.append(lax.ppermute(sent, "kvh", [(i, (i + t) % 4) for i in range(4)]))
        return block, came

    before = lax.ppermute(own[0], "cg", onward)
    w_1 = from_plane(1)
    beside = pass_on(both)
    far = pass_on(query_heads)
    before, own[1] = tie((before, own[1]))
    after = lax.ppermute(own[1], "cg", onward)
    before_beside = pass_on(before)
    before, before_beside, beside, far, w_1, mine_w = tie((before, before_beside, beside, far, w_1, mine_w))
    w_3 = from_plane(3)
    one_1, two_1 = one_way(w_1), other_way(w_1)
    att_0 = attend(near, query_heads, (before, before_beside, both, beside), 0, width)

    att_0, after, w_3, mine_w, far, before = tie((att_0, after, w_3, mine_w, far, before))
    spread_0 = spread(att_0)
    after_beside = pass_on(after)
    w_2 = from_plane(2)
    one_3 = one_way(w_3)
    att_1 = attend(far_meta, far, (before, before_beside, both, beside), 0, width)

    att_1, spread_0, after, after_beside, one_1, two_1, w_1, w_3, one_3 = tie(
        (att_1, spread_0, after, after_beside, one_1, two_1, w_1, w_3, one_3)
    )
    spread_1 = spread(att_1)
    mixed_1 = other_way(jnp.concatenate([one_1, w_3], axis=0))
    kept_0, came_0 = over_z(spread_0)
    att_2 = attend(near, query_heads, (after, after_beside, both, beside), 1, width)

    att_2, came_0, spread_1, one_3, w_2, after = tie((att_2, came_0, spread_1, one_3, w_2, after))
    spread_2 = spread(att_2)
    kept_1, came_1 = over_z(spread_1)
    one_2 = one_way(w_2)
    att_3 = attend(far_meta, far, (after, after_beside, both, beside), 1, width)

    att_3, came_1, spread_2, one_2, mixed_1, one_3, w_2 = tie(
        (att_3, came_1, spread_2, one_2, mixed_1, one_3, w_2)
    )
    spread_3 = spread(att_3)
    kept_2, came_2 = over_z(spread_2)
    mixed_3 = other_way(jnp.concatenate([one_3, w_2], axis=0))
    spread_3, one_2 = tie((spread_3, one_2))
    three_2 = other_way(one_2)

    came_2, w_1, one_1, two_1, mixed_1, w_3, one_3, w_2, one_2 = tie(
        (came_2, w_1, one_1, two_1, mixed_1, w_3, one_3, w_2, one_2)
    )
    came_2, spread_3 = tie((came_2, spread_3))
    level_3 = lax.all_to_all(spread_3, "kvh", split_axis=0, concat_axis=0, tiled=True)
    weights = [
        (w_1, pass_on(w_1), [(1, 0)]),
        (one_1, pass_on(one_1), [(1, 1)]),
        (two_1, pass_on(two_1), [(1, 2)]),
        (mixed_1, pass_on(mixed_1), [(1, 3), (3, 2)]),
        (w_3, pass_on(w_3), [(3, 0)]),
        (one_3, pass_on(one_3), [(3, 1)]),
        (mixed_3, pass_on(mixed_3), [(3, 3), (2, 2)]),
        (w_2, pass_on(w_2), [(2, 0)]),
        (one_2, pass_on(one_2), [(2, 1)]),
        (three_2, pass_on(three_2), [(2, 3)]),
    ]
    parts = []
    for n, (kept, came) in enumerate(((kept_0, came_0), (kept_1, came_1), (kept_2, came_2))):
        parts.append((n // 2, n % 2, 0, kept, level * rows))
        parts += [(n // 2, n % 2, t, block, 0) for t, block in enumerate(came, 1)]
    parts += [(1, 1, lax.rem(level + 4 - z, 4), level_3, z * rows) for z in range(4)]
    return project(parts, out_weight, weights, width)


TILE = 1024


def project_kernel(x_parts, parts, x_at, w_at, *refs):
    n_in = 1 + max(k for k, _ in x_parts)
    x_in, (out_ref, x_ref, w_ref, x_sems, w_sems) = refs[:n_in], refs[-5:]
    w_in, own_w = refs[n_in:-6], refs[-6]
    n_x, n_w = len(x_parts), len(parts)
    step = pl.program_id(0)
    width = x_in[0].shape[1]
    depth = own_w.shape[0] // 8
    own = own_w.shape[0]

    def tile_copies(n, slot):
        cols = pl.ds(pl.multiple_of(n * TILE, TILE), TILE)
        ins = [
            pltpu.make_async_copy(
                w_in[k].at[pl.ds(row, depth), cols],
                w_ref.at[slot, pl.ds(pl.multiple_of(w_at[i], depth), depth), :],
                w_sems.at[slot, i],
            )
            for i, (k, row) in enumerate(parts)
        ]
        ins.append(
            pltpu.make_async_copy(
                own_w.at[:, cols],
                w_ref.at[slot, pl.ds(pl.multiple_of(w_at[n_w], own), own), :],
                w_sems.at[slot, n_w],
            )
        )
        return ins

    def x_copies():
        ins = []
        for i, (k, half) in enumerate(x_parts):
            for p in range(2):
                row = pl.multiple_of(x_at[n_x + i] + p * BLK, BLK)
                to = ((p ^ half) * 2 + p) * BLK
                ins.append(
                    pltpu.make_async_copy(
                        x_in[k].at[pl.ds(row, BLK), :],
                        x_ref.at[pl.ds(to, BLK), pl.ds(pl.multiple_of(x_at[i], width), width)],
                        x_sems.at[i, p],
                    )
                )
        return ins

    slot = lax.rem(step, 2)

    @pl.when(step == 0)
    def _():
        ins = x_copies() + tile_copies(0, 0)
        for copy in ins:
            copy.start()
        for copy in ins[: 2 * n_x]:
            copy.wait()

    @pl.when(step + 1 < pl.num_programs(0))
    def _():
        for copy in tile_copies(step + 1, 1 - slot):
            copy.start()

    for copy in tile_copies(step, slot):
        copy.wait()
    out_ref[...] = jnp.dot(x_ref[...], w_ref[slot], preferred_element_type=jnp.float32).astype(jnp.bfloat16)


def project(found, own_w, weights, width):
    level, chip, core = (lax.axis_index(n) for n in ("kvh", "cg", "cp"))
    groups = own_w.shape[0] // width
    x_in, x_parts, x_col, x_row = [], [], [], []
    for g, half, t, block, row in found:
        place = [k for k, b in enumerate(x_in) if b is block]
        if not place:
            place = [len(x_in)]
            x_in.append(block)
        x_parts.append((place[0], half))
        x_col.append((lax.rem(level + 4 - t, 4) * groups + g) * width)
        x_row.append(row + level * 0)
    w_in, w_row, parts = [], [], []
    depth = own_w.shape[0] // 8
    for *blocks, content in weights:
        for other, block in enumerate(blocks):
            p = core ^ 1 if other else core
            for i, (t, way) in enumerate(content):
                c = chip ^ (p * 0, 1 + p, 2 - p, p * 0 + 3)[way]
                parts.append((len(w_in), i * depth))
                w_row.append(lax.rem(level + 4 - t, 4) * own_w.shape[0] + (c * 2 + p) * depth)
            w_in.append(block)
    w_row.append(level * own_w.shape[0])
    total = own_w.shape[0] * 4
    out = own_w.shape[1]
    rows = 4 * BLK
    return pl.pallas_call(
        functools.partial(project_kernel, x_parts, parts),
        out_shape=jax.ShapeDtypeStruct((rows, out), jnp.bfloat16),
        grid_spec=pltpu.PrefetchScalarGridSpec(
            num_scalar_prefetch=2,
            grid=(out // TILE,),
            in_specs=[pl.BlockSpec(memory_space=pl.ANY)] * (len(x_in) + len(w_in) + 1),
            out_specs=pl.BlockSpec((rows, TILE), lambda n, *_: (0, n)),
            scratch_shapes=[
                pltpu.VMEM((rows, total), jnp.bfloat16),
                pltpu.VMEM((2, total, TILE), jnp.bfloat16),
                pltpu.SemaphoreType.DMA((len(x_parts), 2)),
                pltpu.SemaphoreType.DMA((2, len(parts) + 1)),
            ],
        ),
        compiler_params=pltpu.CompilerParams(vmem_limit_bytes=60 * 1024 * 1024),
        cost_estimate=pl.CostEstimate(
            flops=2 * rows * total * out, bytes_accessed=2 * total * out, transcendentals=0
        ),
    )(jnp.stack(x_col + x_row).astype(jnp.int32), jnp.stack(w_row).astype(jnp.int32), *x_in, *w_in, own_w)


def solution(mesh):
    num_ctx, num_kvh = mesh.devices.shape
    split = Mesh(mesh.devices.reshape(num_ctx // 2, 2, num_kvh), ("cg", "cp", "kvh"))
    placed = (P(CTX, "kvh"), P(CTX, "kvh"), P(CTX, "kvh"), P("kvh", None), P(), P())
    return jax.shard_map(
        body, mesh=split, in_specs=placed, out_specs=P(("cg", "cp", "kvh"), None), check_vma=False
    )
```

```python
import functools
import math
import jax
import jax.numpy as jnp
from jax import lax
from jax.experimental import pallas as pl
from jax.experimental.pallas import tpu as pltpu
from jax.sharding import Mesh, PartitionSpec as P

HEAD_SIZE = 128
BLK = 128
MOST = 4096
CHUNK = 1536
CTX = ("cg", "cp")
SCALE = math.log2(math.e) / HEAD_SIZE**0.5
NEG = -1e30


def attend_kernel(
    group, firsts, lows, p_first, p_last, p_start, q_at, side,
    q_ref, kv0, kv1, kv2, kv3, out_ref,
    kv_ref, q_four, sbuf, top, acc, sems,
):
    step = pl.program_id(0)
    heads = q_ref.shape[1] // HEAD_SIZE
    shard = kv0.shape[0]

    @pl.when(step == 0)
    def _():
        copies = [
            pltpu.make_async_copy(
                src.at[pl.ds(group * shard if i > 1 else 0, shard), :],
                kv_ref.at[pl.ds(pl.multiple_of((i // 2 * 2 + lax.rem(i + side[0], 2)) * shard, BLK), shard), :],
                sems.at[i],
            )
            for i, src in enumerate((kv0, kv1, kv2, kv3))
        ]
        for copy in copies:
            copy.start()
        for copy in copies:
            copy.wait()

    for h in range(heads):
        q_four[h * BLK : (h + 1) * BLK, :] = q_ref[:, h * HEAD_SIZE : (h + 1) * HEAD_SIZE]

    first = firsts[step]
    end = first + BLK
    count = (end - lows[step] + CHUNK - 1) // CHUNK
    pos = first + lax.broadcasted_iota(jnp.int32, (BLK, 1), 0)
    start = lax.fori_loop(
        p_first[step] + 1,
        p_last[step] + 1,
        lambda p, s: jnp.where(p_start[p] <= pos, p_start[p], s),
        jnp.full((BLK, 1), p_start[p_first[step]], jnp.int32),
    )
    latest = p_start[p_last[step]]
    wide = CHUNK // HEAD_SIZE

    def score(j, masked, init):
        begin = end - (j + 1) * CHUNK
        at = pl.multiple_of(jnp.maximum(begin, 0), BLK)
        keys = kv_ref[pl.ds(at, CHUNK), :HEAD_SIZE]
        s = lax.dot_general(
            q_four[...], keys, (((1,), (1,)), ((), ())), preferred_element_type=jnp.float32
        )
        if masked:
            key_pos = at + lax.broadcasted_iota(jnp.int32, (BLK, CHUNK), 1)
            allowed = (key_pos >= start) & (key_pos <= jnp.minimum(pos, begin + CHUNK - 1))
            s = jnp.where(jnp.concatenate([allowed] * heads, axis=0), s, NEG)
        sbuf[j] = s
        m = s[:, :HEAD_SIZE]
        for w in range(1, wide):
            m = jnp.maximum(m, s[:, w * HEAD_SIZE : (w + 1) * HEAD_SIZE])
        top[...] = m if init else jnp.maximum(top[...], m)

    score(0, True, True)

    def first_pass(j, carry):
        full = end - (j + 1) * CHUNK >= latest

        @pl.when(full)
        def _():
            score(j, False, False)

        @pl.when(jnp.logical_not(full))
        def _():
            score(j, True, False)

        return carry

    lax.fori_loop(1, count, first_pass, 0)
    top[...] = jnp.broadcast_to(jnp.max(top[...], axis=1, keepdims=True), top.shape)

    def mix(j, init):
        at = pl.multiple_of(jnp.maximum(end - (j + 1) * CHUNK, 0), BLK)
        values = kv_ref[pl.ds(at, CHUNK), HEAD_SIZE:]
        both = jnp.concatenate([values, jnp.ones_like(values)], axis=1)
        m = jnp.concatenate([top[...]] * wide, axis=1)
        weights = jnp.exp2((sbuf[j] - m) * SCALE).astype(jnp.bfloat16)
        r = jnp.dot(weights, both, preferred_element_type=jnp.float32)
        acc[...] = r if init else acc[...] + r

    mix(0, True)

    def second_pass(j, carry):
        mix(j, False)
        return carry

    lax.fori_loop(1, count, second_pass, 0)
    for h in range(heads):
        rows = slice(h * BLK, (h + 1) * BLK)
        out_ref[:, h * HEAD_SIZE : (h + 1) * HEAD_SIZE] = (
            acc[rows, :HEAD_SIZE] / acc[rows, HEAD_SIZE:]
        ).astype(jnp.bfloat16)


def attend(meta, query, pieces, g, width):
    steps = meta[0].shape[0]
    stacked = BLK * width // HEAD_SIZE
    chunks = (MOST + BLK + CHUNK - 1) // CHUNK
    window = 4 * query.shape[0]
    return pl.pallas_call(
        functools.partial(attend_kernel, g),
        out_shape=jax.ShapeDtypeStruct((steps * BLK, width), jnp.bfloat16),
        grid_spec=pltpu.PrefetchScalarGridSpec(
            num_scalar_prefetch=7,
            grid=(steps,),
            in_specs=[pl.BlockSpec((BLK, width), lambda i, *s: (s[5][i], g))]
            + [pl.BlockSpec(memory_space=pl.ANY)] * 4,
            out_specs=pl.BlockSpec((BLK, width), lambda i, *s: (i, 0)),
            scratch_shapes=[
                pltpu.VMEM((window, 2 * HEAD_SIZE), jnp.bfloat16),
                pltpu.VMEM((stacked, HEAD_SIZE), jnp.bfloat16),
                pltpu.VMEM((chunks, stacked, CHUNK), jnp.float32),
                pltpu.VMEM((stacked, HEAD_SIZE), jnp.float32),
                pltpu.VMEM((stacked, 2 * HEAD_SIZE), jnp.float32),
                pltpu.SemaphoreType.DMA((4,)),
            ],
        ),
        compiler_params=pltpu.CompilerParams(vmem_limit_bytes=60 * 1024 * 1024),
        cost_estimate=pl.CostEstimate(
            flops=4 * steps * BLK * width * 8000,
            bytes_accessed=window * 512,
            transcendentals=steps * BLK * 4 * 2600,
        ),
    )(*meta, query, *pieces)


def body(query_heads, key_heads, value_head_rows, out_weight, piece_lengths, block_order):
    num_ctx = lax.axis_size(CTX)
    num_cg = lax.axis_size("cg")
    num_kvh = lax.axis_size("kvh")
    chip = lax.axis_index("cg")
    core = lax.axis_index("cp")
    shard = query_heads.shape[0]
    block_count = shard // BLK
    per_pair = block_count // num_ctx
    groups = key_heads.shape[1] // HEAD_SIZE
    width = query_heads.shape[1] // groups
    pieces = piece_lengths.shape[0]
    swap = [(0, 1), (1, 0)]
    onward = [(i, i + 1) for i in range(num_cg - 1)]

    def pair_of(keys, values, g):
        cols = slice(g * HEAD_SIZE, (g + 1) * HEAD_SIZE)
        return jnp.concatenate([keys[:, cols], values[:, cols]], axis=1)

    own = [pair_of(key_heads, value_head_rows, g) for g in range(groups)]
    both = jnp.concatenate(own, axis=0)

    table = block_order.reshape(num_ctx, num_cg, 2 * per_pair)
    mine = lax.dynamic_index_in_dim(table, chip, 1, keepdims=False).reshape(num_ctx, per_pair, 2)
    mine = lax.dynamic_index_in_dim(mine, core, 2, keepdims=False)
    if per_pair > 1:
        mine = jnp.where(core == 1, mine[:, ::-1], mine)

    row = lax.broadcasted_iota(jnp.int32, (pieces, pieces), 0)
    column = lax.broadcasted_iota(jnp.int32, (pieces, pieces), 1)
    ends = jnp.sum(jnp.where(column <= row, piece_lengths[None, :], 0), axis=1)
    base = (chip - 1) * (2 * shard)
    p_start = (ends - piece_lengths - base).astype(jnp.int32)

    def meta_of(blocks):
        first_rows = blocks * BLK
        p_first = jnp.sum((ends[None, :] <= first_rows[:, None]).astype(jnp.int32), axis=1)
        p_last = jnp.sum((ends[None, :] <= first_rows[:, None] + BLK - 1).astype(jnp.int32), axis=1)
        lows = jnp.sum(jnp.where(ends[None, :] <= first_rows[:, None], piece_lengths[None, :], 0), axis=1)
        lows = lows // BLK * BLK - base
        parts = (first_rows - base, lows, p_first, p_last, p_start, blocks % block_count, core[None])
        return [a.astype(jnp.int32) for a in parts]

    def spread(attended):
        return lax.all_to_all(attended, CTX, split_axis=0, concat_axis=0, tiled=True)

    if not (num_cg == 4 and num_kvh == 4 and groups == 2 and per_pair == 2):
        weights = lax.all_gather(out_weight, "kvh", axis=0, tiled=True)
        beside = lax.ppermute(both, "cp", swap)
        queries = [query_heads] + [lax.ppermute(query_heads, "cp", swap)] * (per_pair - 1)
        columns = []
        for g in range(groups):
            before = lax.ppermute(own[g], "cg", onward)
            window = [before, lax.ppermute(before, "cp", swap), both, beside]
            found = [attend(meta_of(mine[:, i]), q, window, g, width) for i, q in enumerate(queries)]
            if per_pair > 1:
                found = [jnp.where(core == 1, b, a) for a, b in (found, found[::-1])]
            rows = jnp.stack([f.reshape(num_ctx, BLK, width) for f in found], axis=1)
            rows = spread(rows.reshape(-1, width))
            rows = lax.all_to_all(rows, "kvh", split_axis=0, concat_axis=0, tiled=True)
            columns.append(rows.reshape(num_kvh, 2, per_pair, BLK, width).transpose(2, 1, 3, 0, 4))
        x = jnp.stack(columns, axis=4).reshape(2 * per_pair * BLK, -1)
        return jnp.dot(x, weights, preferred_element_type=jnp.float32).astype(jnp.bfloat16)

    tie = lax.optimization_barrier
    depth = out_weight.shape[0] // 8
    mine_w = lax.dynamic_slice_in_dim(out_weight, (chip * 2 + core) * depth, depth, 0)
    first_way = [(c * 2 + p, (c ^ (1 + p)) * 2 + p) for c in range(4) for p in range(2)]
    second_way = [(c * 2 + p, (c ^ (2 - p)) * 2 + p) for c in range(4) for p in range(2)]

    def from_plane(t):
        return lax.ppermute(mine_w, "kvh", [(i, (i + t) % 4) for i in range(4)])

    def one_way(block):
        return lax.ppermute(block, CTX, first_way)

    def other_way(block):
        return lax.ppermute(block, CTX, second_way)

    def pass_on(block):
        return lax.ppermute(block, "cp", swap)

    near, far_meta = meta_of(mine[:, 0]), meta_of(mine[:, 1])
    level = lax.axis_index("kvh")
    rows = 2 * BLK

    def over_z(block):
        came = []
        for t in range(1, 4):
            sent = lax.dynamic_slice_in_dim(block, lax.rem(level + t, 4) * rows, rows, 0)
            came.append(lax.ppermute(sent, "kvh", [(i, (i + t) % 4) for i in range(4)]))
        return block, came

    before = lax.ppermute(own[0], "cg", onward)
    w_1 = from_plane(1)
    beside = pass_on(both)
    far = pass_on(query_heads)
    before, own[1] = tie((before, own[1]))
    after = lax.ppermute(own[1], "cg", onward)
    before_beside = pass_on(before)
    before, before_beside, beside, far, w_1, mine_w = tie((before, before_beside, beside, far, w_1, mine_w))
    w_3 = from_plane(3)
    one_1, two_1 = one_way(w_1), other_way(w_1)
    att_0 = attend(near, query_heads, (before, before_beside, both, beside), 0, width)

    att_0, after, w_3, mine_w, far, before = tie((att_0, after, w_3, mine_w, far, before))
    spread_0 = spread(att_0)
    after_beside = pass_on(after)
    w_2 = from_plane(2)
    one_3 = one_way(w_3)
    att_1 = attend(far_meta, far, (before, before_beside, both, beside), 0, width)

    att_1, spread_0, after, after_beside, one_1, two_1, w_1, w_3, one_3 = tie(
        (att_1, spread_0, after, after_beside, one_1, two_1, w_1, w_3, one_3)
    )
    spread_1 = spread(att_1)
    mixed_1 = other_way(jnp.concatenate([one_1, w_3], axis=0))
    kept_0, came_0 = over_z(spread_0)
    att_2 = attend(near, query_heads, (after, after_beside, both, beside), 1, width)

    att_2, came_0, spread_1, one_3, w_2, after = tie((att_2, came_0, spread_1, one_3, w_2, after))
    spread_2 = spread(att_2)
    kept_1, came_1 = over_z(spread_1)
    one_2 = one_way(w_2)
    att_3 = attend(far_meta, far, (after, after_beside, both, beside), 1, width)

    att_3, came_1, spread_2, one_2, mixed_1, one_3, w_2 = tie(
        (att_3, came_1, spread_2, one_2, mixed_1, one_3, w_2)
    )
    spread_3 = spread(att_3)
    kept_2, came_2 = over_z(spread_2)
    mixed_3 = other_way(jnp.concatenate([one_3, w_2], axis=0))
    spread_3, one_2 = tie((spread_3, one_2))
    three_2 = other_way(one_2)

    came_2, w_1, one_1, two_1, mixed_1, w_3, one_3, w_2, one_2 = tie(
        (came_2, w_1, one_1, two_1, mixed_1, w_3, one_3, w_2, one_2)
    )
    came_2, spread_3 = tie((came_2, spread_3))
    level_3 = lax.all_to_all(spread_3, "kvh", split_axis=0, concat_axis=0, tiled=True)
    weights = [
        (w_1, pass_on(w_1), [(1, 0)]),
        (one_1, pass_on(one_1), [(1, 1)]),
        (two_1, pass_on(two_1), [(1, 2)]),
        (mixed_1, pass_on(mixed_1), [(1, 3), (3, 2)]),
        (w_3, pass_on(w_3), [(3, 0)]),
        (one_3, pass_on(one_3), [(3, 1)]),
        (mixed_3, pass_on(mixed_3), [(3, 3), (2, 2)]),
        (w_2, pass_on(w_2), [(2, 0)]),
        (one_2, pass_on(one_2), [(2, 1)]),
        (three_2, pass_on(three_2), [(2, 3)]),
    ]
    parts = []
    for n, (kept, came) in enumerate(((kept_0, came_0), (kept_1, came_1), (kept_2, came_2))):
        parts.append((n // 2, n % 2, 0, kept, level * rows))
        parts += [(n // 2, n % 2, t, block, 0) for t, block in enumerate(came, 1)]
    parts += [(1, 1, lax.rem(level + 4 - z, 4), level_3, z * rows) for z in range(4)]
    return project(parts, out_weight, weights, width)


TILE = 1024


def project_kernel(x_parts, parts, x_at, w_at, *refs):
    n_in = 1 + max(k for k, _ in x_parts)
    x_in, (out_ref, x_ref, w_ref, x_sems, w_sems) = refs[:n_in], refs[-5:]
    w_in, own_w = refs[n_in:-6], refs[-6]
    n_x, n_w = len(x_parts), len(parts)
    step = pl.program_id(0)
    width = x_in[0].shape[1]
    depth = own_w.shape[0] // 8
    own = own_w.shape[0]

    def tile_copies(n, slot):
        cols = pl.ds(pl.multiple_of(n * TILE, TILE), TILE)
        ins = [
            pltpu.make_async_copy(
                w_in[k].at[pl.ds(row, depth), cols],
                w_ref.at[slot, pl.ds(pl.multiple_of(w_at[i], depth), depth), :],
                w_sems.at[slot, i],
            )
            for i, (k, row) in enumerate(parts)
        ]
        ins.append(
            pltpu.make_async_copy(
                own_w.at[:, cols],
                w_ref.at[slot, pl.ds(pl.multiple_of(w_at[n_w], own), own), :],
                w_sems.at[slot, n_w],
            )
        )
        return ins

    def x_copies():
        ins = []
        for i, (k, half) in enumerate(x_parts):
            for p in range(2):
                row = pl.multiple_of(x_at[n_x + i] + p * BLK, BLK)
                to = ((p ^ half) * 2 + p) * BLK
                ins.append(
                    pltpu.make_async_copy(
                        x_in[k].at[pl.ds(row, BLK), :],
                        x_ref.at[pl.ds(to, BLK), pl.ds(pl.multiple_of(x_at[i], width), width)],
                        x_sems.at[i, p],
                    )
                )
        return ins

    slot = lax.rem(step, 2)

    @pl.when(step == 0)
    def _():
        ins = x_copies() + tile_copies(0, 0)
        for copy in ins:
            copy.start()
        for copy in ins[: 2 * n_x]:
            copy.wait()

    @pl.when(step + 1 < pl.num_programs(0))
    def _():
        for copy in tile_copies(step + 1, 1 - slot):
            copy.start()

    for copy in tile_copies(step, slot):
        copy.wait()
    out_ref[...] = jnp.dot(x_ref[...], w_ref[slot], preferred_element_type=jnp.float32).astype(jnp.bfloat16)


def project(found, own_w, weights, width):
    level, chip, core = (lax.axis_index(n) for n in ("kvh", "cg", "cp"))
    groups = own_w.shape[0] // width
    x_in, x_parts, x_col, x_row = [], [], [], []
    for g, half, t, block, row in found:
        place = [k for k, b in enumerate(x_in) if b is block]
        if not place:
            place = [len(x_in)]
            x_in.append(block)
        x_parts.append((place[0], half))
        x_col.append((lax.rem(level + 4 - t, 4) * groups + g) * width)
        x_row.append(row + level * 0)
    w_in, w_row, parts = [], [], []
    depth = own_w.shape[0] // 8
    for *blocks, content in weights:
        for other, block in enumerate(blocks):
            p = core ^ 1 if other else core
            for i, (t, way) in enumerate(content):
                c = chip ^ (p * 0, 1 + p, 2 - p, p * 0 + 3)[way]
                parts.append((len(w_in), i * depth))
                w_row.append(lax.rem(level + 4 - t, 4) * own_w.shape[0] + (c * 2 + p) * depth)
            w_in.append(block)
    w_row.append(level * own_w.shape[0])
    total = own_w.shape[0] * 4
    out = own_w.shape[1]
    rows = 4 * BLK
    return pl.pallas_call(
        functools.partial(project_kernel, x_parts, parts),
        out_shape=jax.ShapeDtypeStruct((rows, out), jnp.bfloat16),
        grid_spec=pltpu.PrefetchScalarGridSpec(
            num_scalar_prefetch=2,
            grid=(out // TILE,),
            in_specs=[pl.BlockSpec(memory_space=pl.ANY)] * (len(x_in) + len(w_in) + 1),
            out_specs=pl.BlockSpec((rows, TILE), lambda n, *_: (0, n)),
            scratch_shapes=[
                pltpu.VMEM((rows, total), jnp.bfloat16),
                pltpu.VMEM((2, total, TILE), jnp.bfloat16),
                pltpu.SemaphoreType.DMA((len(x_parts), 2)),
                pltpu.SemaphoreType.DMA((2, len(parts) + 1)),
            ],
        ),
        compiler_params=pltpu.CompilerParams(vmem_limit_bytes=60 * 1024 * 1024),
        cost_estimate=pl.CostEstimate(
            flops=2 * rows * total * out, bytes_accessed=2 * total * out, transcendentals=0
        ),
    )(jnp.stack(x_col + x_row).astype(jnp.int32), jnp.stack(w_row).astype(jnp.int32), *x_in, *w_in, own_w)


def solution(mesh):
    num_ctx, num_kvh = mesh.devices.shape
    split = Mesh(mesh.devices.reshape(num_ctx // 2, 2, num_kvh), ("cg", "cp", "kvh"))
    placed = (P(CTX, "kvh"), P(CTX, "kvh"), P(CTX, "kvh"), P("kvh", None), P(), P())
    return jax.shard_map(
        body, mesh=split, in_specs=placed, out_specs=P(("cg", "cp", "kvh"), None), check_vma=False
    )
```

```python
import functools
import math
import jax
import jax.numpy as jnp
from jax import lax
from jax.experimental import pallas as pl
from jax.experimental.pallas import tpu as pltpu
from jax.sharding import Mesh, PartitionSpec as P

HEAD_SIZE = 128
BLK = 128
MOST = 4096
CHUNK = 1408
CTX = ("cg", "cp")
SCALE = math.log2(math.e) / HEAD_SIZE**0.5
NEG = -1e30


def attend_kernel(
    group, firsts, lows, p_first, p_last, p_start, q_at, side,
    q_ref, kv0, kv1, kv2, kv3, out_ref,
    kv_ref, q_four, sbuf, top, acc, sems,
):
    step = pl.program_id(0)
    heads = q_ref.shape[1] // HEAD_SIZE
    shard = kv0.shape[0]

    @pl.when(step == 0)
    def _():
        copies = [
            pltpu.make_async_copy(
                src.at[pl.ds(group * shard if i > 1 else 0, shard), :],
                kv_ref.at[pl.ds(pl.multiple_of((i // 2 * 2 + lax.rem(i + side[0], 2)) * shard, BLK), shard), :],
                sems.at[i],
            )
            for i, src in enumerate((kv0, kv1, kv2, kv3))
        ]
        for copy in copies:
            copy.start()
        for copy in copies:
            copy.wait()

    for h in range(heads):
        q_four[h * BLK : (h + 1) * BLK, :] = q_ref[:, h * HEAD_SIZE : (h + 1) * HEAD_SIZE]

    first = firsts[step]
    end = first + BLK
    count = (end - lows[step] + CHUNK - 1) // CHUNK
    pos = first + lax.broadcasted_iota(jnp.int32, (BLK, 1), 0)
    start = lax.fori_loop(
        p_first[step] + 1,
        p_last[step] + 1,
        lambda p, s: jnp.where(p_start[p] <= pos, p_start[p], s),
        jnp.full((BLK, 1), p_start[p_first[step]], jnp.int32),
    )
    latest = p_start[p_last[step]]
    wide = CHUNK // HEAD_SIZE

    def score(j, masked, init):
        begin = end - (j + 1) * CHUNK
        at = pl.multiple_of(jnp.maximum(begin, 0), BLK)
        keys = kv_ref[pl.ds(at, CHUNK), :HEAD_SIZE]
        s = lax.dot_general(
            q_four[...], keys, (((1,), (1,)), ((), ())), preferred_element_type=jnp.float32
        )
        if masked:
            key_pos = at + lax.broadcasted_iota(jnp.int32, (BLK, CHUNK), 1)
            allowed = (key_pos >= start) & (key_pos <= jnp.minimum(pos, begin + CHUNK - 1))
            s = jnp.where(jnp.concatenate([allowed] * heads, axis=0), s, NEG)
        sbuf[j] = s
        m = s[:, :HEAD_SIZE]
        for w in range(1, wide):
            m = jnp.maximum(m, s[:, w * HEAD_SIZE : (w + 1) * HEAD_SIZE])
        top[...] = m if init else jnp.maximum(top[...], m)

    score(0, True, True)

    def first_pass(j, carry):
        full = end - (j + 1) * CHUNK >= latest

        @pl.when(full)
        def _():
            score(j, False, False)

        @pl.when(jnp.logical_not(full))
        def _():
            score(j, True, False)

        return carry

    lax.fori_loop(1, count, first_pass, 0)
    top[...] = jnp.broadcast_to(jnp.max(top[...], axis=1, keepdims=True), top.shape)

    def mix(j, init):
        at = pl.multiple_of(jnp.maximum(end - (j + 1) * CHUNK, 0), BLK)
        values = kv_ref[pl.ds(at, CHUNK), HEAD_SIZE:]
        both = jnp.concatenate([values, jnp.ones_like(values)], axis=1)
        m = jnp.concatenate([top[...]] * wide, axis=1)
        weights = jnp.exp2((sbuf[j] - m) * SCALE).astype(jnp.bfloat16)
        r = jnp.dot(weights, both, preferred_element_type=jnp.float32)
        acc[...] = r if init else acc[...] + r

    mix(0, True)

    def second_pass(j, carry):
        mix(j, False)
        return carry

    lax.fori_loop(1, count, second_pass, 0)
    for h in range(heads):
        rows = slice(h * BLK, (h + 1) * BLK)
        out_ref[:, h * HEAD_SIZE : (h + 1) * HEAD_SIZE] = (
            acc[rows, :HEAD_SIZE] / acc[rows, HEAD_SIZE:]
        ).astype(jnp.bfloat16)


def attend(meta, query, pieces, g, width):
    steps = meta[0].shape[0]
    stacked = BLK * width // HEAD_SIZE
    chunks = (MOST + BLK + CHUNK - 1) // CHUNK
    window = 4 * query.shape[0]
    return pl.pallas_call(
        functools.partial(attend_kernel, g),
        out_shape=jax.ShapeDtypeStruct((steps * BLK, width), jnp.bfloat16),
        grid_spec=pltpu.PrefetchScalarGridSpec(
            num_scalar_prefetch=7,
            grid=(steps,),
            in_specs=[pl.BlockSpec((BLK, width), lambda i, *s: (s[5][i], g))]
            + [pl.BlockSpec(memory_space=pl.ANY)] * 4,
            out_specs=pl.BlockSpec((BLK, width), lambda i, *s: (i, 0)),
            scratch_shapes=[
                pltpu.VMEM((window, 2 * HEAD_SIZE), jnp.bfloat16),
                pltpu.VMEM((stacked, HEAD_SIZE), jnp.bfloat16),
                pltpu.VMEM((chunks, stacked, CHUNK), jnp.float32),
                pltpu.VMEM((stacked, HEAD_SIZE), jnp.float32),
                pltpu.VMEM((stacked, 2 * HEAD_SIZE), jnp.float32),
                pltpu.SemaphoreType.DMA((4,)),
            ],
        ),
        compiler_params=pltpu.CompilerParams(vmem_limit_bytes=60 * 1024 * 1024),
        cost_estimate=pl.CostEstimate(
            flops=4 * steps * BLK * width * 8000,
            bytes_accessed=window * 512,
            transcendentals=steps * BLK * 4 * 2600,
        ),
    )(*meta, query, *pieces)


def body(query_heads, key_heads, value_head_rows, out_weight, piece_lengths, block_order):
    num_ctx = lax.axis_size(CTX)
    num_cg = lax.axis_size("cg")
    num_kvh = lax.axis_size("kvh")
    chip = lax.axis_index("cg")
    core = lax.axis_index("cp")
    shard = query_heads.shape[0]
    block_count = shard // BLK
    per_pair = block_count // num_ctx
    groups = key_heads.shape[1] // HEAD_SIZE
    width = query_heads.shape[1] // groups
    pieces = piece_lengths.shape[0]
    swap = [(0, 1), (1, 0)]
    onward = [(i, i + 1) for i in range(num_cg - 1)]

    def pair_of(keys, values, g):
        cols = slice(g * HEAD_SIZE, (g + 1) * HEAD_SIZE)
        return jnp.concatenate([keys[:, cols], values[:, cols]], axis=1)

    own = [pair_of(key_heads, value_head_rows, g) for g in range(groups)]
    both = jnp.concatenate(own, axis=0)

    table = block_order.reshape(num_ctx, num_cg, 2 * per_pair)
    mine = lax.dynamic_index_in_dim(table, chip, 1, keepdims=False).reshape(num_ctx, per_pair, 2)
    mine = lax.dynamic_index_in_dim(mine, core, 2, keepdims=False)
    if per_pair > 1:
        mine = jnp.where(core == 1, mine[:, ::-1], mine)

    row = lax.broadcasted_iota(jnp.int32, (pieces, pieces), 0)
    column = lax.broadcasted_iota(jnp.int32, (pieces, pieces), 1)
    ends = jnp.sum(jnp.where(column <= row, piece_lengths[None, :], 0), axis=1)
    base = (chip - 1) * (2 * shard)
    p_start = (ends - piece_lengths - base).astype(jnp.int32)

    def meta_of(blocks):
        first_rows = blocks * BLK
        p_first = jnp.sum((ends[None, :] <= first_rows[:, None]).astype(jnp.int32), axis=1)
        p_last = jnp.sum((ends[None, :] <= first_rows[:, None] + BLK - 1).astype(jnp.int32), axis=1)
        lows = jnp.sum(jnp.where(ends[None, :] <= first_rows[:, None], piece_lengths[None, :], 0), axis=1)
        lows = lows // BLK * BLK - base
        parts = (first_rows - base, lows, p_first, p_last, p_start, blocks % block_count, core[None])
        return [a.astype(jnp.int32) for a in parts]

    def spread(attended):
        return lax.all_to_all(attended, CTX, split_axis=0, concat_axis=0, tiled=True)

    if not (num_cg == 4 and num_kvh == 4 and groups == 2 and per_pair == 2):
        weights = lax.all_gather(out_weight, "kvh", axis=0, tiled=True)
        beside = lax.ppermute(both, "cp", swap)
        queries = [query_heads] + [lax.ppermute(query_heads, "cp", swap)] * (per_pair - 1)
        columns = []
        for g in range(groups):
            before = lax.ppermute(own[g], "cg", onward)
            window = [before, lax.ppermute(before, "cp", swap), both, beside]
            found = [attend(meta_of(mine[:, i]), q, window, g, width) for i, q in enumerate(queries)]
            if per_pair > 1:
                found = [jnp.where(core == 1, b, a) for a, b in (found, found[::-1])]
            rows = jnp.stack([f.reshape(num_ctx, BLK, width) for f in found], axis=1)
            rows = spread(rows.reshape(-1, width))
            rows = lax.all_to_all(rows, "kvh", split_axis=0, concat_axis=0, tiled=True)
            columns.append(rows.reshape(num_kvh, 2, per_pair, BLK, width).transpose(2, 1, 3, 0, 4))
        x = jnp.stack(columns, axis=4).reshape(2 * per_pair * BLK, -1)
        return jnp.dot(x, weights, preferred_element_type=jnp.float32).astype(jnp.bfloat16)

    tie = lax.optimization_barrier
    depth = out_weight.shape[0] // 8
    mine_w = lax.dynamic_slice_in_dim(out_weight, (chip * 2 + core) * depth, depth, 0)
    first_way = [(c * 2 + p, (c ^ (1 + p)) * 2 + p) for c in range(4) for p in range(2)]
    second_way = [(c * 2 + p, (c ^ (2 - p)) * 2 + p) for c in range(4) for p in range(2)]

    def from_plane(t):
        return lax.ppermute(mine_w, "kvh", [(i, (i + t) % 4) for i in range(4)])

    def one_way(block):
        return lax.ppermute(block, CTX, first_way)

    def other_way(block):
        return lax.ppermute(block, CTX, second_way)

    def pass_on(block):
        return lax.ppermute(block, "cp", swap)

    near, far_meta = meta_of(mine[:, 0]), meta_of(mine[:, 1])
    level = lax.axis_index("kvh")
    rows = 2 * BLK

    def over_z(block):
        came = []
        for t in range(1, 4):
            sent = lax.dynamic_slice_in_dim(block, lax.rem(level + t, 4) * rows, rows, 0)
            came.append(lax.ppermute(sent, "kvh", [(i, (i + t) % 4) for i in range(4)]))
        return block, came

    before = lax.ppermute(own[0], "cg", onward)
    w_1 = from_plane(1)
    beside = pass_on(both)
    far = pass_on(query_heads)
    before, own[1] = tie((before, own[1]))
    after = lax.ppermute(own[1], "cg", onward)
    before_beside = pass_on(before)
    before, before_beside, beside, far, w_1, mine_w = tie((before, before_beside, beside, far, w_1, mine_w))
    w_3 = from_plane(3)
    one_1, two_1 = one_way(w_1), other_way(w_1)
    att_0 = attend(near, query_heads, (before, before_beside, both, beside), 0, width)

    att_0, after, w_3, mine_w, far, before = tie((att_0, after, w_3, mine_w, far, before))
    spread_0 = spread(att_0)
    after_beside = pass_on(after)
    w_2 = from_plane(2)
    one_3 = one_way(w_3)
    att_1 = attend(far_meta, far, (before, before_beside, both, beside), 0, width)

    att_1, spread_0, after, after_beside, one_1, two_1, w_1, w_3, one_3 = tie(
        (att_1, spread_0, after, after_beside, one_1, two_1, w_1, w_3, one_3)
    )
    spread_1 = spread(att_1)
    mixed_1 = other_way(jnp.concatenate([one_1, w_3], axis=0))
    kept_0, came_0 = over_z(spread_0)
    att_2 = attend(near, query_heads, (after, after_beside, both, beside), 1, width)

    att_2, came_0, spread_1, one_3, w_2, after = tie((att_2, came_0, spread_1, one_3, w_2, after))
    spread_2 = spread(att_2)
    kept_1, came_1 = over_z(spread_1)
    one_2 = one_way(w_2)
    att_3 = attend(far_meta, far, (after, after_beside, both, beside), 1, width)

    att_3, came_1, spread_2, one_2, mixed_1, one_3, w_2 = tie(
        (att_3, came_1, spread_2, one_2, mixed_1, one_3, w_2)
    )
    spread_3 = spread(att_3)
    kept_2, came_2 = over_z(spread_2)
    mixed_3 = other_way(jnp.concatenate([one_3, w_2], axis=0))
    spread_3, one_2 = tie((spread_3, one_2))
    three_2 = other_way(one_2)

    came_2, w_1, one_1, two_1, mixed_1, w_3, one_3, w_2, one_2 = tie(
        (came_2, w_1, one_1, two_1, mixed_1, w_3, one_3, w_2, one_2)
    )
    came_2, spread_3 = tie((came_2, spread_3))
    level_3 = lax.all_to_all(spread_3, "kvh", split_axis=0, concat_axis=0, tiled=True)
    weights = [
        (w_1, pass_on(w_1), [(1, 0)]),
        (one_1, pass_on(one_1), [(1, 1)]),
        (two_1, pass_on(two_1), [(1, 2)]),
        (mixed_1, pass_on(mixed_1), [(1, 3), (3, 2)]),
        (w_3, pass_on(w_3), [(3, 0)]),
        (one_3, pass_on(one_3), [(3, 1)]),
        (mixed_3, pass_on(mixed_3), [(3, 3), (2, 2)]),
        (w_2, pass_on(w_2), [(2, 0)]),
        (one_2, pass_on(one_2), [(2, 1)]),
        (three_2, pass_on(three_2), [(2, 3)]),
    ]
    parts = []
    for n, (kept, came) in enumerate(((kept_0, came_0), (kept_1, came_1), (kept_2, came_2))):
        parts.append((n // 2, n % 2, 0, kept, level * rows))
        parts += [(n // 2, n % 2, t, block, 0) for t, block in enumerate(came, 1)]
    parts += [(1, 1, lax.rem(level + 4 - z, 4), level_3, z * rows) for z in range(4)]
    return project(parts, out_weight, weights, width)


TILE = 1024


def project_kernel(x_parts, parts, x_at, w_at, *refs):
    n_in = 1 + max(k for k, _ in x_parts)
    x_in, (out_ref, x_ref, w_ref, x_sems, w_sems) = refs[:n_in], refs[-5:]
    w_in, own_w = refs[n_in:-6], refs[-6]
    n_x, n_w = len(x_parts), len(parts)
    step = pl.program_id(0)
    width = x_in[0].shape[1]
    depth = own_w.shape[0] // 8
    own = own_w.shape[0]

    def tile_copies(n, slot):
        cols = pl.ds(pl.multiple_of(n * TILE, TILE), TILE)
        ins = [
            pltpu.make_async_copy(
                w_in[k].at[pl.ds(row, depth), cols],
                w_ref.at[slot, pl.ds(pl.multiple_of(w_at[i], depth), depth), :],
                w_sems.at[slot, i],
            )
            for i, (k, row) in enumerate(parts)
        ]
        ins.append(
            pltpu.make_async_copy(
                own_w.at[:, cols],
                w_ref.at[slot, pl.ds(pl.multiple_of(w_at[n_w], own), own), :],
                w_sems.at[slot, n_w],
            )
        )
        return ins

    def x_copies():
        ins = []
        for i, (k, half) in enumerate(x_parts):
            for p in range(2):
                row = pl.multiple_of(x_at[n_x + i] + p * BLK, BLK)
                to = ((p ^ half) * 2 + p) * BLK
                ins.append(
                    pltpu.make_async_copy(
                        x_in[k].at[pl.ds(row, BLK), :],
                        x_ref.at[pl.ds(to, BLK), pl.ds(pl.multiple_of(x_at[i], width), width)],
                        x_sems.at[i, p],
                    )
                )
        return ins

    slot = lax.rem(step, 2)

    @pl.when(step == 0)
    def _():
        ins = x_copies() + tile_copies(0, 0)
        for copy in ins:
            copy.start()
        for copy in ins[: 2 * n_x]:
            copy.wait()

    @pl.when(step + 1 < pl.num_programs(0))
    def _():
        for copy in tile_copies(step + 1, 1 - slot):
            copy.start()

    for copy in tile_copies(step, slot):
        copy.wait()
    out_ref[...] = jnp.dot(x_ref[...], w_ref[slot], preferred_element_type=jnp.float32).astype(jnp.bfloat16)


def project(found, own_w, weights, width):
    level, chip, core = (lax.axis_index(n) for n in ("kvh", "cg", "cp"))
    groups = own_w.shape[0] // width
    x_in, x_parts, x_col, x_row = [], [], [], []
    for g, half, t, block, row in found:
        place = [k for k, b in enumerate(x_in) if b is block]
        if not place:
            place = [len(x_in)]
            x_in.append(block)
        x_parts.append((place[0], half))
        x_col.append((lax.rem(level + 4 - t, 4) * groups + g) * width)
        x_row.append(row + level * 0)
    w_in, w_row, parts = [], [], []
    depth = own_w.shape[0] // 8
    for *blocks, content in weights:
        for other, block in enumerate(blocks):
            p = core ^ 1 if other else core
            for i, (t, way) in enumerate(content):
                c = chip ^ (p * 0, 1 + p, 2 - p, p * 0 + 3)[way]
                parts.append((len(w_in), i * depth))
                w_row.append(lax.rem(level + 4 - t, 4) * own_w.shape[0] + (c * 2 + p) * depth)
            w_in.append(block)
    w_row.append(level * own_w.shape[0])
    total = own_w.shape[0] * 4
    out = own_w.shape[1]
    rows = 4 * BLK
    return pl.pallas_call(
        functools.partial(project_kernel, x_parts, parts),
        out_shape=jax.ShapeDtypeStruct((rows, out), jnp.bfloat16),
        grid_spec=pltpu.PrefetchScalarGridSpec(
            num_scalar_prefetch=2,
            grid=(out // TILE,),
            in_specs=[pl.BlockSpec(memory_space=pl.ANY)] * (len(x_in) + len(w_in) + 1),
            out_specs=pl.BlockSpec((rows, TILE), lambda n, *_: (0, n)),
            scratch_shapes=[
                pltpu.VMEM((rows, total), jnp.bfloat16),
                pltpu.VMEM((2, total, TILE), jnp.bfloat16),
                pltpu.SemaphoreType.DMA((len(x_parts), 2)),
                pltpu.SemaphoreType.DMA((2, len(parts) + 1)),
            ],
        ),
        compiler_params=pltpu.CompilerParams(vmem_limit_bytes=60 * 1024 * 1024),
        cost_estimate=pl.CostEstimate(
            flops=2 * rows * total * out, bytes_accessed=2 * total * out, transcendentals=0
        ),
    )(jnp.stack(x_col + x_row).astype(jnp.int32), jnp.stack(w_row).astype(jnp.int32), *x_in, *w_in, own_w)


def solution(mesh):
    num_ctx, num_kvh = mesh.devices.shape
    split = Mesh(mesh.devices.reshape(num_ctx // 2, 2, num_kvh), ("cg", "cp", "kvh"))
    placed = (P(CTX, "kvh"), P(CTX, "kvh"), P(CTX, "kvh"), P("kvh", None), P(), P())
    return jax.shard_map(
        body, mesh=split, in_specs=placed, out_specs=P(("cg", "cp", "kvh"), None), check_vma=False
    )
```
